256 devices in a mesh: gx: 32 (over z, x_hi, core), gy: 8 (over x_lo, y).
Axes of the slice: x: 4 (x_hi: 2, x_lo: 2; x = x_hi * 2 + x_lo), y: 4, z: 8, core: 2. Of those that a mesh axis runs over, the one named last changes fastest.
Arguments:
- field_in: bfloat16 [3, 64, 256, 128], P(None, 'gx', 'gy'), may hold values from -6 to 6
- conv_first: bfloat16 [32, 27, 3], replicated, may hold values from -0.625 to 0.625
- bias_first: float32 [32], replicated, may hold values from -3 to 3
- conv_second: bfloat16 [32, 27, 32], replicated, may hold values from -0.21875 to 0.21875
- cotangent: bfloat16 [32, 64, 256, 128], P(None, 'gx', 'gy'), may hold values from -6 to 6
- mask_first: int32 [32, 64, 256, 128], P(None, 'gx', 'gy'), may hold values 0 or 1
- mask_second: int32 [32, 64, 256, 128], P(None, 'gx', 'gy'), may hold values 0 or 1
Outputs:
- input_grad: float32 [3, 64, 256, 128], P(None, 'gx', 'gy')
- grad_conv_first: float32 [32, 27, 3], P('gx')
- grad_conv_second: float32 [32, 27, 32], P('gx')
The draws below stay inside these ranges and needn't reach their ends.
All inputs are finite; a program needn't handle non-finite values. No bound on the sum of `mask_first` or of `mask_second` on one device may be relied on, other than what follows from the above.
Results may differ from the reference program's by a relative error of at most 0.004.
Values may be sent and summed in bfloat16 or wider, within the bound.
A program may use at most 64 MiB of HBM per device.

```python
import math
import jax
import jax.numpy as jnp
from jax import lax

CIN = 3
CH = 32
NZ = 128
NX = 64
NY = 256


def touch_ends(entries, stream_key, low, high):
    index_at = [jax.random.randint(jax.random.fold_in(stream_key, axis), (), 0, length) for axis, length in enumerate(entries.shape)]
    widest = entries.shape.index(max(entries.shape))
    neighbour = index_at[:widest] + [(index_at[widest] + 1) % entries.shape[widest]] + index_at[widest + 1:]
    return entries.at[tuple(index_at)].set(low).at[tuple(neighbour)].set(high)


def with_spikes(array, own_key, source, target, parts, factor):
    def block_of(dim):
        return (jnp.arange(array.shape[dim]) // (array.shape[dim] // parts)).reshape((-1,) + (1,) * (array.ndim - 1 - dim))

    first = jax.random.permutation(own_key, parts)[block_of(target)]
    second = (block_of(target) + parts // 2) % parts
    return jnp.where((block_of(source) == first) | (block_of(source) == second), factor * array, array)


def block_levels(key, shape, cuts, least, high):
    loudness, own = 1.0, jax.random.fold_in(key, 6)
    for position, shards_of in cuts:
        steps = jnp.exp(jax.random.uniform(jax.random.fold_in(own, position), (shards_of,), jnp.float32, least / len(cuts), high / len(cuts)))
        loudness = loudness * jnp.repeat(steps, shape[position] // shards_of).reshape([-1 if axis == position else 1 for axis in range(len(shape))])
    return loudness


def scatter_about(own_key, extent, scale, reach, pieces=(), kind=jnp.bfloat16):
    values = scale * jax.random.normal(own_key, extent, jnp.float32)
    if pieces:
        values = values * block_levels(own_key, extent, pieces, -0.22, 0.18)
    return jnp.clip(values, -reach, reach).astype(kind)


def bell_draw_with(rng, shape, deviation, limit, cuts, heavy, dtype=jnp.bfloat16):
    values = deviation * jax.random.normal(rng, shape, jnp.float32)
    if cuts:
        values = values * block_levels(rng, shape, cuts, -0.22, 0.18)
    return jnp.clip(with_spikes(values, jax.random.fold_in(rng, 3), *heavy), -limit, limit).astype(dtype)


def setup_inputs(seed: int = 0) -> dict:
    keys = jax.random.split(jax.random.key(seed), 8)
    return {
        "field_in": scatter_about(keys[0], (CIN, NX, NY, NZ), 1.0, 6.0, ((1, 32), (2, 8))),
        "conv_first": scatter_about(keys[1], (CH, 27, CIN), (27 * CIN) ** -0.5, 0.625),
        "bias_first": scatter_about(keys[2], (CH,), 0.5, 3.0, (), jnp.float32),
        "conv_second": scatter_about(keys[3], (CH, 27, CH), (27 * CH) ** -0.5, 0.21875),
        "cotangent": bell_draw_with(keys[4], (CH, NX, NY, NZ), 1.0, 6.0, ((1, 32), (2, 8)), (1, 0, 32, 2.75)),
        "mask_first": touch_ends((jax.random.randint(keys[5], (CH, NX, NY, NZ), 0, 2) < 1).astype(jnp.int32), jax.random.fold_in(keys[5], 1), 0, 1),
        "mask_second": touch_ends((jax.random.randint(keys[6], (CH, NX, NY, NZ), 0, 2) < 1).astype(jnp.int32), jax.random.fold_in(keys[6], 1), 0, 1),
    }


leak_slope = 0.01

def wrap_conv(field_vals, weights):
    out_ch = weights.shape[0]
    in_ch = weights.shape[2]
    padded = jnp.pad(field_vals, ((0, 0), (1, 1), (1, 1), (1, 1)), mode='wrap')
    kernel = weights.reshape(out_ch, 3, 3, 3, in_ch).transpose(0, 4, 1, 2, 3)
    result = lax.conv_general_dilated(padded[None], kernel, (1, 1, 1), 'VALID', dimension_numbers=('NCDHW', 'OIDHW', 'NCDHW'), precision=lax.Precision.HIGHEST)
    return result[0]

def flipped(weights):
    return weights[:, ::-1, :].transpose(2, 1, 0)

def weight_grad(grad_vals, field_vals):
    columns = []
    for tap_x in range(3):
        for tap_y in range(3):
            for tap_z in range(3):
                shifted = jnp.roll(field_vals, (1 - tap_x, 1 - tap_y, 1 - tap_z), axis=(1, 2, 3))
                columns.append(jnp.einsum('oxyz,cxyz->oc', grad_vals, shifted, precision=lax.Precision.HIGHEST))
    return jnp.stack(columns, axis=1)

def reference(field_in, conv_first, bias_first, conv_second, cotangent, mask_first, mask_second):
    field_f = field_in.astype(jnp.float32)
    first_w = conv_first.astype(jnp.float32)
    second_w = conv_second.astype(jnp.float32)
    pre_act = wrap_conv(field_f, first_w) + bias_first.astype(jnp.float32)[:, None, None, None]
    hidden = jnp.where(pre_act >= 0, pre_act, leak_slope * pre_act).astype(jnp.bfloat16)
    factor_second = jnp.where(mask_second == 1, 1.0, leak_slope).astype(jnp.float32)
    cot_masked = (cotangent.astype(jnp.float32) * factor_second).astype(jnp.bfloat16)
    grad_hidden = wrap_conv(cot_masked.astype(jnp.float32), flipped(second_w))
    factor_first = jnp.where(mask_first == 1, 1.0, leak_slope).astype(jnp.float32)
    grad_masked = (grad_hidden * factor_first).astype(jnp.bfloat16)
    input_grad = wrap_conv(grad_masked.astype(jnp.float32), flipped(first_w))
    norm_scale = 1.0 / math.sqrt(NX * NY * NZ)
    grad_second = weight_grad(cot_masked.astype(jnp.float32), hidden.astype(jnp.float32)) * norm_scale
    grad_first = weight_grad(grad_masked.astype(jnp.float32), field_f) * norm_scale
    return (input_grad, grad_first, grad_second)
```

```python
import functools
import math

import jax
import jax.numpy as jnp
from jax import lax
from jax.experimental import pallas as pl
from jax.experimental.pallas import tpu as pltpu
from jax.sharding import PartitionSpec as P

MESH = pl.DeviceIdType.MESH
SLOPE = 0.01
F32 = jnp.float32
BF16 = jnp.bfloat16
NT = (((1,), (1,)), ((), ()))


def factor(mask):
    return jnp.where(mask == 1, 1.0, SLOPE).astype(F32)


def shift(values, amount):
    return pltpu.roll(values, amount % 128, 1) if amount else values


def pair_of_rows(ref, planes, row):
    sides = []
    for side in range(2):
        blocks = []
        for plane in planes:
            block = ref[plane, pl.ds(row + side, 3)]
            blocks.append(block.reshape(block.shape[0] * block.shape[1], block.shape[2]))
        sides.append(jnp.concatenate(blocks, axis=0))
    return jnp.concatenate(sides, axis=1)


def kernel(
    nx, ny, scale,
    cot_in, mask1_in, mask2_in, field_in, a1, a2, a3, bias,
    grad_out, weights_out,
    cot_raw, mask1, mask2, field_raw, pad_cot, factors, pad_field, hid3, grad, acc2, acc1,
    part, part_x, got_x, got_y, got_c, mine, got_gx, row_sum, got_gy,
    local_sem, f_send, f_recv, p_send, p_recv, o_send, o_recv, s1_send, s1_recv, s2_send, s2_recv,
):
    gx = lax.axis_index("gx")
    gy = lax.axis_index("gy")

    loads = [
        pltpu.make_async_copy(cot_in, cot_raw, local_sem.at[0]),
        pltpu.make_async_copy(mask2_in, mask2, local_sem.at[1]),
        pltpu.make_async_copy(field_in, field_raw.at[:, 1:3, 16:48], local_sem.at[2]),
        pltpu.make_async_copy(mask1_in, mask1, local_sem.at[3]),
    ]
    for load in loads:
        load.start()

    left, right = lax.rem(gx + nx - 1, nx), lax.rem(gx + 1, nx)
    down, up = lax.rem(gy + ny - 1, ny), lax.rem(gy + 1, ny)

    barrier = pltpu.get_barrier_semaphore()

    def greet_x(k, _):
        pl.semaphore_signal(barrier, inc=1, device_id=(lax.rem(gx + k, nx), gy), device_id_type=MESH)
        return 0

    def greet_y(k, _):
        pl.semaphore_signal(barrier, inc=1, device_id=(gx, lax.rem(gy + k, ny)), device_id_type=MESH)
        return 0

    lax.fori_loop(1, nx, greet_x, 0)
    lax.fori_loop(1, ny, greet_y, 0)
    for corner in ((left, down), (left, up), (right, down), (right, up)):
        pl.semaphore_signal(barrier, inc=1, device_id=corner, device_id_type=MESH)

    loads[0].wait()
    loads[1].wait()
    for x in range(2):
        for half in range(2):
            rows = slice(16 * half, 16 * half + 16)
            values = cot_raw[:, x, rows, :].astype(F32) * factor(mask2[:, x, rows, :])
            pad_cot[x + 1, 1 + 16 * half : 17 + 16 * half] = jnp.swapaxes(values, 0, 1).astype(BF16)

    pl.semaphore_wait(barrier, (nx - 1) + (ny - 1) + 4)

    def remote(src, dst, send, recv, where):
        return pltpu.make_async_remote_copy(
            src_ref=src, dst_ref=dst, send_sem=send, recv_sem=recv, device_id=where, device_id_type=MESH
        )

    places = [(left, gy), (right, gy), (gx, down), (gx, up), (left, down), (left, up), (right, down), (right, up)]
    low, high = slice(0, 16), slice(16, 32)
    inner = slice(16, 48)
    field_moves = [
        (field_in.at[:, 0:1], field_raw.at[:, 3:4, inner]),
        (field_in.at[:, 1:2], field_raw.at[:, 0:1, inner]),
        (field_in.at[:, :, low], field_raw.at[:, 1:3, 48:64]),
        (field_in.at[:, :, high], field_raw.at[:, 1:3, 0:16]),
        (field_in.at[:, 0:1, low], field_raw.at[:, 3:4, 48:64]),
        (field_in.at[:, 0:1, high], field_raw.at[:, 3:4, 0:16]),
        (field_in.at[:, 1:2, low], field_raw.at[:, 0:1, 48:64]),
        (field_in.at[:, 1:2, high], field_raw.at[:, 0:1, 0:16]),
    ]
    cot_moves = [
        (pad_cot.at[1:2, 1:33], pad_cot.at[3:4, 1:33]),
        (pad_cot.at[2:3, 1:33], pad_cot.at[0:1, 1:33]),
        (pad_cot.at[1:3, 1:2], pad_cot.at[1:3, 33:34]),
        (pad_cot.at[1:3, 32:33], pad_cot.at[1:3, 0:1]),
        (pad_cot.at[1:2, 1:2], pad_cot.at[3:4, 33:34]),
        (pad_cot.at[1:2, 32:33], pad_cot.at[3:4, 0:1]),
        (pad_cot.at[2:3, 1:2], pad_cot.at[0:1, 33:34]),
        (pad_cot.at[2:3, 32:33], pad_cot.at[0:1, 0:1]),
    ]
    field_copies = [
        remote(src, dst, f_send.at[i], f_recv.at[i], places[i]) for i, (src, dst) in enumerate(field_moves)
    ]
    cot_copies = [
        remote(src, dst, p_send.at[i], p_recv.at[i], places[i]) for i, (src, dst) in enumerate(cot_moves)
    ]
    for copy in field_copies:
        copy.start()
    for copy in cot_copies:
        copy.start()

    loads[3].wait()
    for x in range(2):
        for half in range(2):
            rows = slice(16 * half, 16 * half + 16)
            factors[x, rows] = jnp.swapaxes(factor(mask1[:, x, rows, :]), 0, 1)

    loads[2].wait()
    for copy in field_copies:
        copy.wait_recv()

    def spread(plane, _):
        for block in range(4):
            rows = []
            for channel in range(3):
                row = field_raw[channel, plane, 16 * block : 16 * block + 16, :].astype(F32)
                rows.extend([shift(row, 1), row, shift(row, -1)])
            rows.extend([jnp.zeros((16, 128), F32)] * 7)
            pad_field[plane, 16 * block : 16 * block + 16] = jnp.swapaxes(jnp.stack(rows, axis=0), 0, 1).astype(BF16)
        return 0

    lax.fori_loop(0, 4, spread, 0)

    def forward(i, _):
        rhs = pair_of_rows(pad_field, range(4), 2 * i + 15)
        pre = jnp.dot(a1[...], rhs, preferred_element_type=F32) + bias[...]
        act = jnp.where(pre >= 0, pre, SLOPE * pre).astype(BF16).astype(F32)
        for x in range(2):
            for tap in range(3):
                for side in range(2):
                    block = shift(act[32 * x : 32 * x + 32, 128 * side : 128 * side + 128], 1 - tap)
                    hid3[i, x, 32 * tap : 32 * tap + 32, 128 * side : 128 * side + 128] = block.astype(BF16)
        return 0

    lax.fori_loop(0, 16, forward, 0)

    for x in range(2):
        for rows in (slice(0, 2), slice(34, 36)):
            grad[x, rows] = jnp.zeros((2, 32, 128), BF16)
    acc2[...] = jnp.zeros_like(acc2)
    acc1[...] = jnp.zeros_like(acc1)
    mine[...] = jnp.zeros_like(mine)

    for copy in cot_copies:
        copy.wait_recv()

    def second(i, _):
        rows = pair_of_rows(pad_cot, range(4), 2 * i)
        total = lax.dot_general(rows[0:288], hid3[i, 0], NT, preferred_element_type=F32)
        total += lax.dot_general(rows[96:384], hid3[i, 1], NT, preferred_element_type=F32)
        acc2[...] += total
        return 0

    lax.fori_loop(0, 16, second, 0)
    for tap in range(9):
        mine[:, tap, 0:96] = acc2[32 * tap : 32 * tap + 32, :]

    def backward(i, _):
        rows = pair_of_rows(pad_cot, range(4), 2 * i)
        out = jnp.dot(a2[...], rows, preferred_element_type=F32)
        for x in range(2):
            for side in range(2):
                total = None
                for tap in range(3):
                    start = 96 * x + 32 * tap
                    term = shift(out[start : start + 32, 128 * side : 128 * side + 128], tap - 1)
                    total = term if total is None else total + term
                grad[x, 2 * i + side + 2] = (total * factors[x, 2 * i + side]).astype(BF16)
        return 0

    lax.fori_loop(0, 16, backward, 0)

    def first(i, _):
        rows = pair_of_rows(pad_field, range(4), 2 * i + 15)
        total = None
        for x in range(2):
            cells = jnp.concatenate([grad[x, 2 * i + 2], grad[x, 2 * i + 3]], axis=1)
            term = lax.dot_general(cells, rows[48 * x : 48 * x + 144], NT, preferred_element_type=F32)
            total = term if total is None else total + term
        acc1[...] += total
        return 0

    lax.fori_loop(0, 16, first, 0)
    mine[:, 9, :] = acc1[:, 0:128]
    mine[:, 10, 0:16] = acc1[:, 128:144]

    def send_row(k, _):
        to = lax.rem(gx + k, nx)
        remote(mine.at[to], got_gx.at[k], s1_send.at[k], s1_recv.at[k], (to, gy)).start()
        return 0

    lax.fori_loop(1, nx, send_row, 0)

    def scatter(i, _):
        rows = pair_of_rows(grad, range(2), 2 * i)
        out = jnp.dot(a3[...], rows, preferred_element_type=F32)
        for plane in range(4):
            for side in range(2):
                total = None
                for tap in range(3):
                    start = 24 * plane + 8 * tap
                    term = shift(out[start : start + 8, 128 * side : 128 * side + 128], tap - 1)
                    total = term if total is None else total + term
                part[plane, 2 * i + side] = total
        return 0

    lax.fori_loop(0, 17, scatter, 0)
    part_x[0] = jnp.swapaxes(part[0, 1:33], 0, 1)[0:3]
    part_x[1] = jnp.swapaxes(part[3, 1:33], 0, 1)[0:3]

    part_moves = [
        (part_x.at[0], got_x.at[1]),
        (part_x.at[1], got_x.at[0]),
        (part.at[1:3, 0], got_y.at[1]),
        (part.at[1:3, 33], got_y.at[0]),
        (part.at[0, 0], got_c.at[3]),
        (part.at[0, 33], got_c.at[2]),
        (part.at[3, 0], got_c.at[1]),
        (part.at[3, 33], got_c.at[0]),
    ]
    part_copies = [
        remote(src, dst, o_send.at[i], o_recv.at[i], places[i]) for i, (src, dst) in enumerate(part_moves)
    ]
    for copy in part_copies:
        copy.start()

    def take_row(k, total):
        to = lax.rem(gx + k, nx)
        remote(mine.at[to], got_gx.at[k], s1_send.at[k], s1_recv.at[k], (to, gy)).wait_recv()
        return total + got_gx[k]

    row_sum[...] = lax.fori_loop(1, nx, take_row, mine[gx])

    def send_sum(k, _):
        to = lax.rem(gy + k, ny)
        remote(row_sum, got_gy.at[k], s2_send.at[k], s2_recv.at[k], (gx, to)).start()
        return 0

    lax.fori_loop(1, ny, send_sum, 0)

    for copy in part_copies:
        copy.wait_recv()
    for x in range(2):
        part[x + 1, 1] += got_y[0, x]
        part[x + 1, 32] += got_y[1, x]
        part[x + 1, 1] += got_c[2 * x]
        part[x + 1, 32] += got_c[2 * x + 1]
    for x in range(2):
        grad_out[:, x] = jnp.swapaxes(part[x + 1, 1:33], 0, 1)[0:3] + got_x[x]

    def take_sum(k, total):
        to = lax.rem(gy + k, ny)
        remote(row_sum, got_gy.at[k], s2_send.at[k], s2_recv.at[k], (gx, to)).wait_recv()
        return total + got_gy[k]

    weights_out[...] = lax.fori_loop(1, ny, take_sum, row_sum[...]) * scale

    for copy in field_copies + cot_copies + part_copies:
        copy.wait_send()

    def sent_row(k, _):
        to = lax.rem(gx + k, nx)
        remote(mine.at[to], got_gx.at[k], s1_send.at[k], s1_recv.at[k], (to, gy)).wait_send()
        return 0

    def sent_sum(k, _):
        to = lax.rem(gy + k, ny)
        remote(row_sum, got_gy.at[k], s2_send.at[k], s2_recv.at[k], (gx, to)).wait_send()
        return 0

    lax.fori_loop(1, nx, sent_row, 0)
    lax.fori_loop(1, ny, sent_sum, 0)


def weight_forms(conv_first, conv_second):
    first = conv_first.reshape(32, 3, 3, 3, 3)
    second = conv_second.reshape(32, 3, 3, 3, 32)
    w1 = jnp.pad(first.transpose(0, 1, 2, 4, 3).reshape(32, 9, 9), ((0, 0), (0, 0), (0, 7))).reshape(32, 144)
    a1 = jnp.concatenate([jnp.pad(w1, ((0, 0), (0, 48))), jnp.pad(w1, ((0, 0), (48, 0)))], axis=0)
    w2 = second[:, ::-1, ::-1].transpose(3, 4, 1, 2, 0).reshape(96, 288)
    a2 = jnp.concatenate([jnp.pad(w2, ((0, 0), (0, 96))), jnp.pad(w2, ((0, 0), (96, 0)))], axis=0)
    w3 = jnp.pad(first[:, :, ::-1].transpose(1, 3, 4, 2, 0), ((0, 0), (0, 0), (0, 5), (0, 0), (0, 0))).reshape(3, 24, 96)
    none = jnp.zeros((24, 96), BF16)
    a3 = jnp.concatenate(
        [
            jnp.concatenate([w3[p - g] if 0 <= p - g < 3 else none for g in range(2)], axis=1)
            for p in range(4)
        ],
        axis=0,
    )
    return a1, a2, a3


def on_device(nx, ny, field_in, conv_first, bias_first, conv_second, cotangent, mask_first, mask_second):
    a1, a2, a3 = weight_forms(conv_first, conv_second)
    bias = jnp.broadcast_to(jnp.concatenate([bias_first, bias_first])[:, None], (64, 256))
    scale = 1.0 / math.sqrt(2 * nx * 32 * ny * 128)
    anywhere = pl.BlockSpec(memory_space=pl.ANY)
    vmem = pl.BlockSpec(memory_space=pltpu.VMEM)
    dma = pltpu.SemaphoreType.DMA
    input_grad, weights = pl.pallas_call(
        functools.partial(kernel, nx, ny, scale),
        out_shape=(
            jax.ShapeDtypeStruct((3, 2, 32, 128), F32),
            jax.ShapeDtypeStruct((11, 128), F32),
        ),
        in_specs=[anywhere] * 4 + [vmem] * 4,
        out_specs=(vmem, vmem),
        scratch_shapes=[
            pltpu.VMEM((32, 2, 32, 128), BF16),
            pltpu.VMEM((32, 2, 32, 128), jnp.int32),
            pltpu.VMEM((32, 2, 32, 128), jnp.int32),
            pltpu.VMEM((3, 4, 64, 128), BF16),
            pltpu.VMEM((4, 34, 32, 128), BF16),
            pltpu.VMEM((2, 32, 32, 128), F32),
            pltpu.VMEM((4, 64, 16, 128), BF16),
            pltpu.VMEM((16, 2, 96, 256), BF16),
            pltpu.VMEM((2, 36, 32, 128), BF16),
            pltpu.VMEM((288, 96), F32),
            pltpu.VMEM((32, 144), F32),
            pltpu.VMEM((4, 34, 8, 128), F32),
            pltpu.VMEM((2, 3, 32, 128), F32),
            pltpu.VMEM((2, 3, 32, 128), F32),
            pltpu.VMEM((2, 2, 8, 128), F32),
            pltpu.VMEM((4, 8, 128), F32),
            pltpu.VMEM((32, 11, 128), F32),
            pltpu.VMEM((nx, 11, 128), F32),
            pltpu.VMEM((11, 128), F32),
            pltpu.VMEM((ny, 11, 128), F32),
            dma((4,)),
            dma((8,)),
            dma((8,)),
            dma((8,)),
            dma((8,)),
            dma((8,)),
            dma((8,)),
            dma((nx,)),
            dma((nx,)),
            dma((ny,)),
            dma((ny,)),
        ],
        compiler_params=pltpu.CompilerParams(
            collective_id=0, has_side_effects=True, vmem_limit_bytes=40 * 1024 * 1024
        ),
    )(cotangent, mask_first, mask_second, field_in, a1, a2, a3, bias)
    grad_second = weights[0:9, 0:96].reshape(3, 3, 3, 32)[::-1, ::-1].reshape(1, 27, 32)
    tail = jnp.concatenate([weights[9], weights[10, 0:16]]).reshape(9, 16)[:, 0:9]
    grad_first = tail.reshape(9, 3, 3).transpose(0, 2, 1).reshape(1, 27, 3)
    return input_grad, grad_first, grad_second


def solution(mesh):
    cells = P(None, "gx", "gy", None)
    return jax.shard_map(
        functools.partial(on_device, mesh.shape["gx"], mesh.shape["gy"]),
        mesh=mesh,
        in_specs=(cells, P(), P(), P(), cells, cells, cells),
        out_specs=(cells, P("gx", None, None), P("gx", None, None)),
        check_vma=False,
    )
```

```python
import functools
import math

import jax
import jax.numpy as jnp
from jax import lax
from jax.experimental import pallas as pl
from jax.experimental.pallas import tpu as pltpu
from jax.sharding import PartitionSpec as P

MESH = pl.DeviceIdType.MESH
SLOPE = 0.01
F32 = jnp.float32
BF16 = jnp.bfloat16
NT = (((1,), (1,)), ((), ()))


def factor(mask):
    return jnp.where(mask == 1, 1.0, SLOPE).astype(F32)


def shift(values, amount):
    return pltpu.roll(values, amount % 128, 1) if amount else values


def beside(ref, planes, row, count):
    sides = []
    for side in range(count):
        blocks = []
        for plane in planes:
            block = ref[plane, pl.ds(row + side, 3)]
            blocks.append(block.reshape(block.shape[0] * block.shape[1], block.shape[2]))
        sides.append(jnp.concatenate(blocks, axis=0) if len(blocks) > 1 else blocks[0])
    return jnp.concatenate(sides, axis=1)


def kernel(
    nx, ny, scale,
    cot_in, mask1_in, mask2_in, field_in, first_in, second_in, bias_in,
    grad_out, first_out, second_out,
    cot_raw, mask1, mask2, field_raw, first_raw, second_raw, bias_raw,
    pad_cot, factors, pad_field, hid3, grad, hidden_grad, acc2, acc1,
    form1, form2, form2_far, form3, turn2, turn3, bias,
    part, part_x, got_x, got_y, got_c, mine, got_gx, row_sum, got_gy,
    local_sem, f_send, f_recv, p_send, p_recv, o_send, o_recv, s1_send, s1_recv, s2_send, s2_recv,
):
    gx = lax.axis_index("gx")
    gy = lax.axis_index("gy")

    loads = [
        pltpu.make_async_copy(cot_in, cot_raw, local_sem.at[0]),
        pltpu.make_async_copy(mask2_in, mask2, local_sem.at[1]),
        pltpu.make_async_copy(field_in, field_raw.at[:, 1:3, 16:48], local_sem.at[2]),
        pltpu.make_async_copy(mask1_in, mask1, local_sem.at[3]),
        pltpu.make_async_copy(first_in, first_raw, local_sem.at[4]),
        pltpu.make_async_copy(second_in, second_raw, local_sem.at[5]),
        pltpu.make_async_copy(bias_in, bias_raw, local_sem.at[6]),
    ]
    for load in loads:
        load.start()

    left, right = lax.rem(gx + nx - 1, nx), lax.rem(gx + 1, nx)
    down, up = lax.rem(gy + ny - 1, ny), lax.rem(gy + 1, ny)

    barrier = pltpu.get_barrier_semaphore()

    def greet_x(k, _):
        pl.semaphore_signal(barrier, inc=1, device_id=(lax.rem(gx + k, nx), gy), device_id_type=MESH)
        return 0

    def greet_y(k, _):
        pl.semaphore_signal(barrier, inc=1, device_id=(gx, lax.rem(gy + k, ny)), device_id_type=MESH)
        return 0

    for corner in ((left, down), (left, up), (right, down), (right, up)):
        pl.semaphore_signal(barrier, inc=1, device_id=corner, device_id_type=MESH)
    lax.fori_loop(1, nx, greet_x, 0)
    lax.fori_loop(1, ny, greet_y, 0)

    loads[0].wait()
    loads[1].wait()
    for x in range(2):
        for half in range(2):
            rows = slice(16 * half, 16 * half + 16)
            values = cot_raw[:, x, rows, :].astype(F32) * factor(mask2[:, x, rows, :])
            pad_cot[x + 1, 1 + 16 * half : 17 + 16 * half] = jnp.swapaxes(values, 0, 1).astype(BF16)

    loads[2].wait()
    pl.semaphore_wait(barrier, (nx - 1) + (ny - 1) + 4)

    def remote(src, dst, send, recv, where):
        return pltpu.make_async_remote_copy(
            src_ref=src, dst_ref=dst, send_sem=send, recv_sem=recv, device_id=where, device_id_type=MESH
        )

    places = [(left, gy), (right, gy), (gx, down), (gx, up), (left, down), (left, up), (right, down), (right, up)]
    low, high = slice(16, 32), slice(32, 48)
    inner, before, after = slice(16, 48), slice(0, 16), slice(48, 64)
    field_moves = [
        (field_raw.at[:, 1:2, inner], field_raw.at[:, 3:4, inner]),
        (field_raw.at[:, 2:3, inner], field_raw.at[:, 0:1, inner]),
        (field_raw.at[:, 1:3, low], field_raw.at[:, 1:3, after]),
        (field_raw.at[:, 1:3, high], field_raw.at[:, 1:3, before]),
        (field_raw.at[:, 1:2, low], field_raw.at[:, 3:4, after]),
        (field_raw.at[:, 1:2, high], field_raw.at[:, 3:4, before]),
        (field_raw.at[:, 2:3, low], field_raw.at[:, 0:1, after]),
        (field_raw.at[:, 2:3, high], field_raw.at[:, 0:1, before]),
    ]
    cot_moves = [
        (pad_cot.at[1:2, 1:33], pad_cot.at[3:4, 1:33]),
        (pad_cot.at[2:3, 1:33], pad_cot.at[0:1, 1:33]),
        (pad_cot.at[1:3, 1:2], pad_cot.at[1:3, 33:34]),
        (pad_cot.at[1:3, 32:33], pad_cot.at[1:3, 0:1]),
        (pad_cot.at[1:2, 1:2], pad_cot.at[3:4, 33:34]),
        (pad_cot.at[1:2, 32:33], pad_cot.at[3:4, 0:1]),
        (pad_cot.at[2:3, 1:2], pad_cot.at[0:1, 33:34]),
        (pad_cot.at[2:3, 32:33], pad_cot.at[0:1, 0:1]),
    ]
    field_copies = [
        remote(src, dst, f_send.at[i], f_recv.at[i], places[i]) for i, (src, dst) in enumerate(field_moves)
    ]
    cot_copies = [
        remote(src, dst, p_send.at[i], p_recv.at[i], places[i]) for i, (src, dst) in enumerate(cot_moves)
    ]
    for copy in cot_copies[2:4] + field_copies + cot_copies[0:2] + cot_copies[4:8]:
        copy.start()

    loads[4].wait()
    loads[5].wait()
    loads[6].wait()
    form1[...] = jnp.zeros_like(form1)
    form2[...] = jnp.zeros_like(form2)
    form2_far[...] = jnp.zeros_like(form2_far)
    form3[...] = jnp.zeros_like(form3)
    turn2[...] = jnp.zeros_like(turn2)
    turn3[...] = jnp.zeros_like(turn3)
    taps1 = jnp.swapaxes(first_raw[...].astype(F32), 0, 1)
    taps2 = jnp.swapaxes(second_raw[...].astype(F32), 0, 1)
    for q in range(9):
        dx, dy = q // 3, q % 3
        back2 = 32 * (8 - q)
        back3 = 32 * (3 * dx + 2 - dy)
        for dz in range(3):
            form1[0:32, 16 * q + 3 * dz : 16 * q + 3 * dz + 3] = taps1[3 * q + dz]
            turn2[back2 : back2 + 32, 32 * dz : 32 * dz + 32] = taps2[3 * q + dz]
            turn3[back3 : back3 + 32, 8 * dz : 8 * dz + 3] = taps1[3 * q + dz]
    form1[32:64, 48:192] = form1[0:32, 0:144]
    whole2 = jnp.transpose(turn2[...])[0:96].astype(BF16)
    form2[0:96, 0:192] = whole2[:, 96:288]
    form2[96:192, 0:192] = whole2[:, 0:192]
    form2_far[0:96, 0:96] = whole2[:, 0:96]
    form2_far[96:192, 96:192] = whole2[:, 192:288]
    whole3 = jnp.transpose(turn3[...])[0:24]
    for plane in range(4):
        for x in range(2):
            if 0 <= plane - x < 3:
                form3[24 * plane : 24 * plane + 24, 96 * x : 96 * x + 96] = whole3[:, 96 * (plane - x) : 96 * (plane - x) + 96]
    across = jnp.transpose(jnp.broadcast_to(bias_raw[...], (8, 128)))[0:32, 0:1]
    bias[0:32] = jnp.broadcast_to(across, (32, 128))
    bias[32:64] = jnp.broadcast_to(across, (32, 128))

    loads[3].wait()
    for x in range(2):
        for half in range(2):
            rows = slice(16 * half, 16 * half + 16)
            factors[x, rows] = jnp.swapaxes(factor(mask1[:, x, rows, :]), 0, 1)

    for x in range(2):
        for rows in (slice(0, 2), slice(34, 36)):
            grad[x, rows] = jnp.zeros((2, 32, 128), BF16)
    mine[...] = jnp.zeros_like(mine)

    def turned(out, x, side):
        total = None
        for tap in range(3):
            start = 96 * x + 32 * tap
            term = shift(out[start : start + 32, 128 * side : 128 * side + 128], tap - 1)
            total = term if total is None else total + term
        return total

    cot_copies[2].wait_recv()
    cot_copies[3].wait_recv()

    def backward_near(i, _):
        out = jnp.dot(form2[...], beside(pad_cot, (1, 2), 8 * i, 8), preferred_element_type=F32)
        for x in range(2):
            for side in range(8):
                hidden_grad[x, 8 * i + side] = turned(out, x, side)
        return 0

    lax.fori_loop(0, 4, backward_near, 0)

    for copy in field_copies:
        copy.wait_recv()

    def spread(plane, _):
        for block in range(4):
            rows = []
            for dz in range(3):
                for channel in range(3):
                    row = field_raw[channel, plane, 16 * block : 16 * block + 16, :].astype(F32)
                    rows.append(shift(row, 1 - dz))
            rows.extend([jnp.zeros((16, 128), F32)] * 7)
            pad_field[plane, 16 * block : 16 * block + 16] = jnp.swapaxes(jnp.stack(rows, axis=0), 0, 1).astype(BF16)
        return 0

    lax.fori_loop(0, 4, spread, 0)
    form1_now = form1[...].astype(BF16)

    def forward(i, _):
        pre = jnp.dot(form1_now, beside(pad_field, range(4), 8 * i + 15, 8), preferred_element_type=F32)
        for x in range(2):
            for side in range(8):
                act = pre[32 * x : 32 * x + 32, 128 * side : 128 * side + 128] + bias[0:32]
                act = jnp.where(act >= 0, act, SLOPE * act).astype(BF16).astype(F32)
                for tap in range(3):
                    hid3[i, x, 32 * tap : 32 * tap + 32, 128 * side : 128 * side + 128] = shift(act, 1 - tap).astype(BF16)
        return 0

    lax.fori_loop(0, 4, forward, 0)

    acc2[...] = jnp.zeros_like(acc2)

    def second_near(i, _):
        rows = beside(pad_cot, (1, 2), 8 * i, 8)
        acc2[96:288] += lax.dot_general(rows, hid3[i, 0], NT, preferred_element_type=F32)
        acc2[0:192] += lax.dot_general(rows, hid3[i, 1], NT, preferred_element_type=F32)
        return 0

    lax.fori_loop(0, 4, second_near, 0)

    for copy in cot_copies[0:2] + cot_copies[4:8]:
        copy.wait_recv()

    def far(i, _):
        rows = beside(pad_cot, (0, 3), 8 * i, 8)
        acc2[0:96] += lax.dot_general(rows[0:96], hid3[i, 0], NT, preferred_element_type=F32)
        acc2[192:288] += lax.dot_general(rows[96:192], hid3[i, 1], NT, preferred_element_type=F32)
        out = jnp.dot(form2_far[...], rows, preferred_element_type=F32)
        for x in range(2):
            for side in range(8):
                total = hidden_grad[x, 8 * i + side] + turned(out, x, side)
                grad[x, 8 * i + side + 2] = (total * factors[x, 8 * i + side]).astype(BF16)
        return 0

    lax.fori_loop(0, 4, far, 0)

    acc1[...] = jnp.zeros_like(acc1)

    def first(i, _):
        rows = beside(pad_field, range(4), 8 * i + 15, 8)
        total = None
        for x in range(2):
            cells = jnp.concatenate([grad[x, 8 * i + 2 + side] for side in range(8)], axis=1)
            term = lax.dot_general(cells, rows[48 * x : 48 * x + 144], NT, preferred_element_type=F32)
            total = term if total is None else total + term
        acc1[...] += total
        return 0

    lax.fori_loop(0, 4, first, 0)
    for q in range(9):
        mine[:, q, 0:96] = acc2[32 * (8 - q) : 32 * (8 - q) + 32, :]
        mine[:, q, 96:105] = acc1[:, 16 * q : 16 * q + 9]

    def send_row(k, _):
        to = lax.rem(gx + k, nx)
        remote(mine.at[to], got_gx.at[k], s1_send.at[k], s1_recv.at[k], (to, gy)).start()
        return 0

    lax.fori_loop(1, nx, send_row, 0)

    form3_now = form3[...].astype(BF16)

    def scatter_rows(row, count):
        out = jnp.dot(form3_now, beside(grad, range(2), row, count), preferred_element_type=F32)
        for plane in range(4):
            for side in range(count):
                total = None
                for tap in range(3):
                    start = 24 * plane + 8 * tap
                    term = shift(out[start : start + 8, 128 * side : 128 * side + 128], tap - 1)
                    total = term if total is None else total + term
                part[plane, row + side] = total

    def scatter(i, _):
        scatter_rows(8 * i, 8)
        return 0

    lax.fori_loop(0, 4, scatter, 0)
    scatter_rows(32, 2)
    part_x[0] = jnp.swapaxes(part[0, 1:33], 0, 1)[0:3]
    part_x[1] = jnp.swapaxes(part[3, 1:33], 0, 1)[0:3]

    part_moves = [
        (part_x.at[0], got_x.at[1]),
        (part_x.at[1], got_x.at[0]),
        (part.at[1:3, 0], got_y.at[1]),
        (part.at[1:3, 33], got_y.at[0]),
        (part.at[0, 0], got_c.at[3]),
        (part.at[0, 33], got_c.at[2]),
        (part.at[3, 0], got_c.at[1]),
        (part.at[3, 33], got_c.at[0]),
    ]
    part_copies = [
        remote(src, dst, o_send.at[i], o_recv.at[i], places[i]) for i, (src, dst) in enumerate(part_moves)
    ]
    for copy in part_copies:
        copy.start()

    def take_row(k, total):
        to = lax.rem(gx + k, nx)
        remote(mine.at[to], got_gx.at[k], s1_send.at[k], s1_recv.at[k], (to, gy)).wait_recv()
        return total + got_gx[k]

    row_sum[...] = lax.fori_loop(1, nx, take_row, mine[gx])

    def send_sum(k, _):
        to = lax.rem(gy + k, ny)
        remote(row_sum, got_gy.at[k], s2_send.at[k], s2_recv.at[k], (gx, to)).start()
        return 0

    lax.fori_loop(1, ny, send_sum, 0)

    for copy in part_copies:
        copy.wait_recv()
    for x in range(2):
        part[x + 1, 1] += got_y[0, x]
        part[x + 1, 32] += got_y[1, x]
        part[x + 1, 1] += got_c[2 * x]
        part[x + 1, 32] += got_c[2 * x + 1]
    for x in range(2):
        grad_out[:, x] = jnp.swapaxes(part[x + 1, 1:33], 0, 1)[0:3] + got_x[x]

    def sent_row(k, _):
        to = lax.rem(gx + k, nx)
        remote(mine.at[to], got_gx.at[k], s1_send.at[k], s1_recv.at[k], (to, gy)).wait_send()
        return 0

    for copy in field_copies + cot_copies + part_copies:
        copy.wait_send()
    lax.fori_loop(1, nx, sent_row, 0)

    def take_sum(k, total):
        to = lax.rem(gy + k, ny)
        remote(row_sum, got_gy.at[k], s2_send.at[k], s2_recv.at[k], (gx, to)).wait_recv()
        return total + got_gy[k]

    total = lax.fori_loop(1, ny, take_sum, row_sum[...]) * scale
    for q in range(9):
        for dz in range(3):
            row = slice(3 * q + dz, 3 * q + dz + 1)
            second_out[0, row] = total[q : q + 1, 32 * dz : 32 * dz + 32]
            first_out[0, row] = total[q : q + 1, 96 + 3 * dz : 96 + 3 * dz + 3]

    def sent_sum(k, _):
        to = lax.rem(gy + k, ny)
        remote(row_sum, got_gy.at[k], s2_send.at[k], s2_recv.at[k], (gx, to)).wait_send()
        return 0

    lax.fori_loop(1, ny, sent_sum, 0)


def on_device(nx, ny, field_in, conv_first, bias_first, conv_second, cotangent, mask_first, mask_second):
    scale = 1.0 / math.sqrt(2 * nx * 32 * ny * 128)
    bias_row = jnp.pad(bias_first.reshape(1, 32), ((0, 0), (0, 96)))
    anywhere = pl.BlockSpec(memory_space=pl.ANY)
    vmem = pl.BlockSpec(memory_space=pltpu.VMEM)
    dma = pltpu.SemaphoreType.DMA
    input_grad, grad_first, grad_second = pl.pallas_call(
        functools.partial(kernel, nx, ny, scale),
        out_shape=(
            jax.ShapeDtypeStruct((3, 2, 32, 128), F32),
            jax.ShapeDtypeStruct((1, 27, 3), F32),
            jax.ShapeDtypeStruct((1, 27, 32), F32),
        ),
        in_specs=[anywhere] * 7,
        out_specs=(vmem, vmem, vmem),
        scratch_shapes=[
            pltpu.VMEM((32, 2, 32, 128), BF16),
            pltpu.VMEM((32, 2, 32, 128), jnp.int32),
            pltpu.VMEM((32, 2, 32, 128), jnp.int32),
            pltpu.VMEM((3, 4, 64, 128), BF16),
            pltpu.VMEM((32, 27, 3), BF16),
            pltpu.VMEM((32, 27, 32), BF16),
            pltpu.VMEM((1, 128), F32),
            pltpu.VMEM((4, 34, 32, 128), BF16),
            pltpu.VMEM((2, 32, 32, 128), F32),
            pltpu.VMEM((4, 64, 16, 128), BF16),
            pltpu.VMEM((4, 2, 96, 1024), BF16),
            pltpu.VMEM((2, 36, 32, 128), BF16),
            pltpu.VMEM((2, 32, 32, 128), F32),
            pltpu.VMEM((288, 96), F32),
            pltpu.VMEM((32, 144), F32),
            pltpu.VMEM((64, 192), F32),
            pltpu.VMEM((192, 192), BF16),
            pltpu.VMEM((192, 192), BF16),
            pltpu.VMEM((96, 192), F32),
            pltpu.VMEM((384, 128), F32),
            pltpu.VMEM((384, 128), F32),
            pltpu.VMEM((64, 128), F32),
            pltpu.VMEM((4, 34, 8, 128), F32),
            pltpu.VMEM((2, 3, 32, 128), F32),
            pltpu.VMEM((2, 3, 32, 128), F32),
            pltpu.VMEM((2, 2, 8, 128), F32),
            pltpu.VMEM((4, 8, 128), F32),
            pltpu.VMEM((32, 9, 128), F32),
            pltpu.VMEM((nx, 9, 128), F32),
            pltpu.VMEM((9, 128), F32),
            pltpu.VMEM((ny, 9, 128), F32),
            dma((7,)),
            dma((8,)),
            dma((8,)),
            dma((8,)),
            dma((8,)),
            dma((8,)),
            dma((8,)),
            dma((nx,)),
            dma((nx,)),
            dma((ny,)),
            dma((ny,)),
        ],
        compiler_params=pltpu.CompilerParams(
            collective_id=0, has_side_effects=True, vmem_limit_bytes=40 * 1024 * 1024
        ),
    )(cotangent, mask_first, mask_second, field_in, conv_first, conv_second, bias_row)
    return input_grad, grad_first, grad_second


def solution(mesh):
    cells = P(None, "gx", "gy", None)
    return jax.shard_map(
        functools.partial(on_device, mesh.shape["gx"], mesh.shape["gy"]),
        mesh=mesh,
        in_specs=(cells, P(), P(), P(), cells, cells, cells),
        out_specs=(cells, P("gx", None, None), P("gx", None, None)),
        check_vma=False,
    )
```

```python
import functools
import math

import jax
import jax.numpy as jnp
from jax import lax
from jax.experimental import pallas as pl
from jax.experimental.pallas import tpu as pltpu
from jax.sharding import PartitionSpec as P

MESH = pl.DeviceIdType.MESH
SLOPE = 0.01
F32 = jnp.float32
BF16 = jnp.bfloat16
NT = (((1,), (1,)), ((), ()))


def factor(mask):
    return jnp.where(mask == 1, 1.0, SLOPE).astype(F32)


def shift(values, amount):
    return pltpu.roll(values, amount % 128, 1) if amount else values


def beside(ref, planes, row, count):
    sides = []
    for side in range(count):
        blocks = []
        for plane in planes:
            block = ref[plane, pl.ds(row + side, 3)]
            blocks.append(block.reshape(block.shape[0] * block.shape[1], block.shape[2]))
        sides.append(jnp.concatenate(blocks, axis=0) if len(blocks) > 1 else blocks[0])
    return jnp.concatenate(sides, axis=1)


def kernel(
    nx, ny, scale,
    cot_in, mask1_in, mask2_in, field_in, first_in, second_in, bias_in,
    grad_out, first_out, second_out,
    cot_raw, mask1, mask2, field_raw, first_raw, second_raw, bias_raw,
    pad_cot, factors, pad_field, hid3, grad, hidden_grad, acc2, acc1,
    form1, form2, form2_far, form3, turn2, turn3, bias,
    part, part_x, got_x, got_y, got_c, mine, got_gx, row_sum, got_gy,
    local_sem, f_send, f_recv, p_send, p_recv, o_send, o_recv, s1_send, s1_recv, s2_send, s2_recv,
):
    gx = lax.axis_index("gx")
    gy = lax.axis_index("gy")

    loads = [
        pltpu.make_async_copy(cot_in, cot_raw, local_sem.at[0]),
        pltpu.make_async_copy(mask2_in, mask2, local_sem.at[1]),
        pltpu.make_async_copy(field_in, field_raw.at[:, 1:3, 16:48], local_sem.at[2]),
        pltpu.make_async_copy(mask1_in, mask1, local_sem.at[3]),
        pltpu.make_async_copy(first_in, first_raw, local_sem.at[4]),
        pltpu.make_async_copy(second_in, second_raw, local_sem.at[5]),
        pltpu.make_async_copy(bias_in, bias_raw, local_sem.at[6]),
    ]
    for load in loads:
        load.start()

    left, right = lax.rem(gx + nx - 1, nx), lax.rem(gx + 1, nx)
    down, up = lax.rem(gy + ny - 1, ny), lax.rem(gy + 1, ny)

    barrier = pltpu.get_barrier_semaphore()

    def greet_x(k, _):
        pl.semaphore_signal(barrier, inc=1, device_id=(lax.rem(gx + k, nx), gy), device_id_type=MESH)
        return 0

    def greet_y(k, _):
        pl.semaphore_signal(barrier, inc=1, device_id=(gx, lax.rem(gy + k, ny)), device_id_type=MESH)
        return 0

    for corner in ((left, down), (left, up), (right, down), (right, up)):
        pl.semaphore_signal(barrier, inc=1, device_id=corner, device_id_type=MESH)
    lax.fori_loop(1, nx, greet_x, 0)
    lax.fori_loop(1, ny, greet_y, 0)

    loads[0].wait()
    loads[1].wait()
    for x in range(2):
        for half in range(2):
            rows = slice(16 * half, 16 * half + 16)
            values = cot_raw[:, x, rows, :].astype(F32) * factor(mask2[:, x, rows, :])
            pad_cot[x + 1, 1 + 16 * half : 17 + 16 * half] = jnp.swapaxes(values, 0, 1).astype(BF16)

    loads[2].wait()
    pl.semaphore_wait(barrier, (nx - 1) + (ny - 1) + 4)

    def remote(src, dst, send, recv, where):
        return pltpu.make_async_remote_copy(
            src_ref=src, dst_ref=dst, send_sem=send, recv_sem=recv, device_id=where, device_id_type=MESH
        )

    places = [(left, gy), (right, gy), (gx, down), (gx, up), (left, down), (left, up), (right, down), (right, up)]
    low, high = slice(16, 32), slice(32, 48)
    inner, before, after = slice(16, 48), slice(0, 16), slice(48, 64)
    field_moves = [
        (field_raw.at[:, 1:2, inner], field_raw.at[:, 3:4, inner]),
        (field_raw.at[:, 2:3, inner], field_raw.at[:, 0:1, inner]),
        (field_raw.at[:, 1:3, low], field_raw.at[:, 1:3, after]),
        (field_raw.at[:, 1:3, high], field_raw.at[:, 1:3, before]),
        (field_raw.at[:, 1:2, low], field_raw.at[:, 3:4, after]),
        (field_raw.at[:, 1:2, high], field_raw.at[:, 3:4, before]),
        (field_raw.at[:, 2:3, low], field_raw.at[:, 0:1, after]),
        (field_raw.at[:, 2:3, high], field_raw.at[:, 0:1, before]),
    ]
    cot_moves = [
        (pad_cot.at[1:2, 1:33], pad_cot.at[3:4, 1:33]),
        (pad_cot.at[2:3, 1:33], pad_cot.at[0:1, 1:33]),
        (pad_cot.at[1:3, 1:2], pad_cot.at[1:3, 33:34]),
        (pad_cot.at[1:3, 32:33], pad_cot.at[1:3, 0:1]),
        (pad_cot.at[1:2, 1:2], pad_cot.at[3:4, 33:34]),
        (pad_cot.at[1:2, 32:33], pad_cot.at[3:4, 0:1]),
        (pad_cot.at[2:3, 1:2], pad_cot.at[0:1, 33:34]),
        (pad_cot.at[2:3, 32:33], pad_cot.at[0:1, 0:1]),
    ]
    field_copies = [
        remote(src, dst, f_send.at[i], f_recv.at[i], places[i]) for i, (src, dst) in enumerate(field_moves)
    ]
    cot_copies = [
        remote(src, dst, p_send.at[i], p_recv.at[i], places[i]) for i, (src, dst) in enumerate(cot_moves)
    ]
    for copy in cot_copies[2:4] + field_copies + cot_copies[0:2] + cot_copies[4:8]:
        copy.start()

    loads[4].wait()
    loads[5].wait()
    loads[6].wait()
    form1[...] = jnp.zeros_like(form1)
    form2[...] = jnp.zeros_like(form2)
    form2_far[...] = jnp.zeros_like(form2_far)
    form3[...] = jnp.zeros_like(form3)
    turn2[...] = jnp.zeros_like(turn2)
    turn3[...] = jnp.zeros_like(turn3)
    for q in range(9):
        dx, dy = q // 3, q % 3
        back2 = 32 * (8 - q)
        back3 = 32 * (3 * dx + 2 - dy)
        for dz in range(3):
            turn2[back2 : back2 + 32, 32 * dz : 32 * dz + 32] = second_raw[3 * q + dz].astype(F32)
        for channel in range(3):
            taps = first_raw[channel].astype(F32)[:, 3 * q : 3 * q + 3]
            form1[0:32, 16 * q + 3 * channel : 16 * q + 3 * channel + 3] = taps
            for dz in range(3):
                turn3[back3 : back3 + 32, 8 * dz + channel : 8 * dz + channel + 1] = taps[:, dz : dz + 1]
    form1[32:64, 48:192] = form1[0:32, 0:144]
    whole2 = jnp.transpose(turn2[...])[0:96].astype(BF16)
    form2[0:96, 0:192] = whole2[:, 96:288]
    form2[96:192, 0:192] = whole2[:, 0:192]
    form2_far[0:96, 0:96] = whole2[:, 0:96]
    form2_far[96:192, 96:192] = whole2[:, 192:288]
    whole3 = jnp.transpose(turn3[...])[0:24]
    for plane in range(4):
        for x in range(2):
            if 0 <= plane - x < 3:
                form3[24 * plane : 24 * plane + 24, 96 * x : 96 * x + 96] = whole3[:, 96 * (plane - x) : 96 * (plane - x) + 96]
    bias[...] = jnp.zeros_like(bias)
    bias[0:8, 0:32] = jnp.broadcast_to(bias_raw[...], (8, 32))
    bias[...] = jnp.broadcast_to(jnp.transpose(bias[0:8])[0:32, 0:1], (32, 128))

    loads[3].wait()
    for x in range(2):
        for half in range(2):
            rows = slice(16 * half, 16 * half + 16)
            factors[x, rows] = jnp.swapaxes(factor(mask1[:, x, rows, :]), 0, 1)

    for x in range(2):
        for rows in (slice(0, 2), slice(34, 36)):
            grad[x, rows] = jnp.zeros((2, 32, 128), BF16)
    mine[...] = jnp.zeros_like(mine)

    def turned(out, x, side):
        total = None
        for tap in range(3):
            start = 96 * x + 32 * tap
            term = shift(out[start : start + 32, 128 * side : 128 * side + 128], tap - 1)
            total = term if total is None else total + term
        return total

    cot_copies[2].wait_recv()
    cot_copies[3].wait_recv()

    def backward_near(i, _):
        out = jnp.dot(form2[...], beside(pad_cot, (1, 2), 8 * i, 8), preferred_element_type=F32)
        for x in range(2):
            for side in range(8):
                hidden_grad[x, 8 * i + side] = turned(out, x, side)
        return 0

    lax.fori_loop(0, 4, backward_near, 0)

    for copy in field_copies:
        copy.wait_recv()

    def spread(plane, _):
        for block in range(4):
            rows = []
            for channel in range(3):
                for dz in range(3):
                    row = field_raw[channel, plane, 16 * block : 16 * block + 16, :].astype(F32)
                    rows.append(shift(row, 1 - dz))
            rows.extend([jnp.zeros((16, 128), F32)] * 7)
            pad_field[plane, 16 * block : 16 * block + 16] = jnp.swapaxes(jnp.stack(rows, axis=0), 0, 1).astype(BF16)
        return 0

    lax.fori_loop(0, 4, spread, 0)
    form1_now = form1[...].astype(BF16)

    def forward(i, _):
        pre = jnp.dot(form1_now, beside(pad_field, range(4), 8 * i + 15, 8), preferred_element_type=F32)
        for x in range(2):
            for side in range(8):
                act = pre[32 * x : 32 * x + 32, 128 * side : 128 * side + 128] + bias[...]
                act = jnp.where(act >= 0, act, SLOPE * act).astype(BF16).astype(F32)
                for tap in range(3):
                    hid3[i, x, 32 * tap : 32 * tap + 32, 128 * side : 128 * side + 128] = shift(act, 1 - tap).astype(BF16)
        return 0

    lax.fori_loop(0, 4, forward, 0)

    acc2[...] = jnp.zeros_like(acc2)

    def second_near(i, _):
        rows = beside(pad_cot, (1, 2), 8 * i, 8)
        acc2[96:288] += lax.dot_general(rows, hid3[i, 0], NT, preferred_element_type=F32)
        acc2[0:192] += lax.dot_general(rows, hid3[i, 1], NT, preferred_element_type=F32)
        return 0

    lax.fori_loop(0, 4, second_near, 0)

    for copy in cot_copies[0:2] + cot_copies[4:8]:
        copy.wait_recv()

    def far(i, _):
        rows = beside(pad_cot, (0, 3), 8 * i, 8)
        acc2[0:96] += lax.dot_general(rows[0:96], hid3[i, 0], NT, preferred_element_type=F32)
        acc2[192:288] += lax.dot_general(rows[96:192], hid3[i, 1], NT, preferred_element_type=F32)
        out = jnp.dot(form2_far[...], rows, preferred_element_type=F32)
        for x in range(2):
            for side in range(8):
                total = hidden_grad[x, 8 * i + side] + turned(out, x, side)
                grad[x, 8 * i + side + 2] = (total * factors[x, 8 * i + side]).astype(BF16)
        return 0

    lax.fori_loop(0, 4, far, 0)

    acc1[...] = jnp.zeros_like(acc1)

    def first(i, _):
        rows = beside(pad_field, range(4), 8 * i + 15, 8)
        total = None
        for x in range(2):
            cells = jnp.concatenate([grad[x, 8 * i + 2 + side] for side in range(8)], axis=1)
            term = lax.dot_general(cells, rows[48 * x : 48 * x + 144], NT, preferred_element_type=F32)
            total = term if total is None else total + term
        acc1[...] += total
        return 0

    lax.fori_loop(0, 4, first, 0)
    for q in range(9):
        mine[:, q, 0:96] = acc2[32 * (8 - q) : 32 * (8 - q) + 32, :]
        mine[:, q, 96:105] = acc1[:, 16 * q : 16 * q + 9]

    def send_row(k, _):
        to = lax.rem(gx + k, nx)
        remote(mine.at[to], got_gx.at[k], s1_send.at[k], s1_recv.at[k], (to, gy)).start()
        return 0

    lax.fori_loop(1, nx, send_row, 0)

    form3_now = form3[...].astype(BF16)

    def scatter_rows(row, count):
        out = jnp.dot(form3_now, beside(grad, range(2), row, count), preferred_element_type=F32)
        for plane in range(4):
            for side in range(count):
                total = None
                for tap in range(3):
                    start = 24 * plane + 8 * tap
                    term = shift(out[start : start + 8, 128 * side : 128 * side + 128], tap - 1)
                    total = term if total is None else total + term
                part[plane, row + side] = total

    def scatter(i, _):
        scatter_rows(8 * i, 8)
        return 0

    lax.fori_loop(0, 4, scatter, 0)
    scatter_rows(32, 2)
    part_x[0] = jnp.swapaxes(part[0, 1:33], 0, 1)[0:3]
    part_x[1] = jnp.swapaxes(part[3, 1:33], 0, 1)[0:3]

    part_moves = [
        (part_x.at[0], got_x.at[1]),
        (part_x.at[1], got_x.at[0]),
        (part.at[1:3, 0], got_y.at[1]),
        (part.at[1:3, 33], got_y.at[0]),
        (part.at[0, 0], got_c.at[3]),
        (part.at[0, 33], got_c.at[2]),
        (part.at[3, 0], got_c.at[1]),
        (part.at[3, 33], got_c.at[0]),
    ]
    part_copies = [
        remote(src, dst, o_send.at[i], o_recv.at[i], places[i]) for i, (src, dst) in enumerate(part_moves)
    ]
    for copy in part_copies:
        copy.start()

    def take_row(k, total):
        to = lax.rem(gx + k, nx)
        remote(mine.at[to], got_gx.at[k], s1_send.at[k], s1_recv.at[k], (to, gy)).wait_recv()
        return total + got_gx[k]

    row_sum[...] = lax.fori_loop(1, nx, take_row, mine[gx])

    def send_sum(k, _):
        to = lax.rem(gy + k, ny)
        remote(row_sum, got_gy.at[k], s2_send.at[k], s2_recv.at[k], (gx, to)).start()
        return 0

    lax.fori_loop(1, ny, send_sum, 0)

    for copy in part_copies:
        copy.wait_recv()
    for x in range(2):
        part[x + 1, 1] += got_y[0, x]
        part[x + 1, 32] += got_y[1, x]
        part[x + 1, 1] += got_c[2 * x]
        part[x + 1, 32] += got_c[2 * x + 1]
    for x in range(2):
        grad_out[:, x] = jnp.swapaxes(part[x + 1, 1:33], 0, 1)[0:3] + got_x[x]

    def sent_row(k, _):
        to = lax.rem(gx + k, nx)
        remote(mine.at[to], got_gx.at[k], s1_send.at[k], s1_recv.at[k], (to, gy)).wait_send()
        return 0

    for copy in field_copies + cot_copies + part_copies:
        copy.wait_send()
    lax.fori_loop(1, nx, sent_row, 0)

    def take_sum(k, total):
        to = lax.rem(gy + k, ny)
        remote(row_sum, got_gy.at[k], s2_send.at[k], s2_recv.at[k], (gx, to)).wait_recv()
        return total + got_gy[k]

    total = lax.fori_loop(1, ny, take_sum, row_sum[...]) * scale
    for q in range(9):
        for dz in range(3):
            second_out[3 * q + dz] = total[q : q + 1, 32 * dz : 32 * dz + 32]
        for channel in range(3):
            first_out[channel, :, 3 * q : 3 * q + 3] = total[q : q + 1, 96 + 3 * channel : 96 + 3 * channel + 3]

    def sent_sum(k, _):
        to = lax.rem(gy + k, ny)
        remote(row_sum, got_gy.at[k], s2_send.at[k], s2_recv.at[k], (gx, to)).wait_send()
        return 0

    lax.fori_loop(1, ny, sent_sum, 0)


def put_out(a, b, c, a_out, b_out, c_out, sem):
    copies = [
        pltpu.make_async_copy(src, dst, sem.at[i]) for i, (src, dst) in enumerate(((a, a_out), (b, b_out), (c, c_out)))
    ]
    for copy in copies:
        copy.start()
    for copy in copies:
        copy.wait()


def on_device(nx, ny, field_in, conv_first, bias_first, conv_second, cotangent, mask_first, mask_second):
    scale = 1.0 / math.sqrt(2 * nx * 32 * ny * 128)
    outside = pl.BlockSpec(memory_space=pltpu.HBM)
    anywhere = pl.BlockSpec(memory_space=pl.ANY)
    vmem = pl.BlockSpec(memory_space=pltpu.VMEM)
    dma = pltpu.SemaphoreType.DMA
    results = pl.pallas_call(
        functools.partial(kernel, nx, ny, scale),
        out_shape=(
            jax.ShapeDtypeStruct((3, 2, 32, 128), F32),
            jax.ShapeDtypeStruct((3, 1, 27), F32),
            jax.ShapeDtypeStruct((27, 1, 32), F32),
        ),
        in_specs=[outside] * 7,
        out_specs=(vmem, vmem, vmem),
        scratch_shapes=[
            pltpu.VMEM((32, 2, 32, 128), BF16),
            pltpu.VMEM((32, 2, 32, 128), jnp.int32),
            pltpu.VMEM((32, 2, 32, 128), jnp.int32),
            pltpu.VMEM((3, 4, 64, 128), BF16),
            pltpu.VMEM((3, 32, 27), BF16),
            pltpu.VMEM((27, 32, 32), BF16),
            pltpu.VMEM((1, 32), F32),
            pltpu.VMEM((4, 34, 32, 128), BF16),
            pltpu.VMEM((2, 32, 32, 128), F32),
            pltpu.VMEM((4, 64, 16, 128), BF16),
            pltpu.VMEM((4, 2, 96, 1024), BF16),
            pltpu.VMEM((2, 36, 32, 128), BF16),
            pltpu.VMEM((2, 32, 32, 128), F32),
            pltpu.VMEM((288, 96), F32),
            pltpu.VMEM((32, 144), F32),
            pltpu.VMEM((64, 192), F32),
            pltpu.VMEM((192, 192), BF16),
            pltpu.VMEM((192, 192), BF16),
            pltpu.VMEM((96, 192), F32),
            pltpu.VMEM((384, 128), F32),
            pltpu.VMEM((384, 128), F32),
            pltpu.VMEM((32, 128), F32),
            pltpu.VMEM((4, 34, 8, 128), F32),
            pltpu.VMEM((2, 3, 32, 128), F32),
            pltpu.VMEM((2, 3, 32, 128), F32),
            pltpu.VMEM((2, 2, 8, 128), F32),
            pltpu.VMEM((4, 8, 128), F32),
            pltpu.VMEM((32, 9, 128), F32),
            pltpu.VMEM((nx, 9, 128), F32),
            pltpu.VMEM((9, 128), F32),
            pltpu.VMEM((ny, 9, 128), F32),
            dma((7,)),
            dma((8,)),
            dma((8,)),
            dma((8,)),
            dma((8,)),
            dma((8,)),
            dma((8,)),
            dma((nx,)),
            dma((nx,)),
            dma((ny,)),
            dma((ny,)),
        ],
        compiler_params=pltpu.CompilerParams(
            collective_id=0, has_side_effects=True, vmem_limit_bytes=60 * 1024 * 1024
        ),
    )(
        cotangent, mask_first, mask_second, field_in,
        conv_first.transpose(2, 0, 1), conv_second.transpose(1, 0, 2), bias_first.reshape(1, 32),
    )
    input_grad, grad_first, grad_second = pl.pallas_call(
        put_out,
        out_shape=tuple(jax.ShapeDtypeStruct(r.shape, r.dtype) for r in results),
        in_specs=[anywhere] * 3,
        out_specs=(outside,) * 3,
        scratch_shapes=[dma((3,))],
    )(*results)
    return input_grad, grad_first.transpose(1, 2, 0), grad_second.transpose(1, 0, 2)


def solution(mesh):
    cells = P(None, "gx", "gy", None)
    return jax.shard_map(
        functools.partial(on_device, mesh.shape["gx"], mesh.shape["gy"]),
        mesh=mesh,
        in_specs=(cells, P(), P(), P(), cells, cells, cells),
        out_specs=(cells, P("gx", None, None), P("gx", None, None)),
        check_vma=False,
    )
```

```python
import functools
import math

import jax
import jax.numpy as jnp
from jax import lax
from jax.experimental import pallas as pl
from jax.experimental.pallas import tpu as pltpu
from jax.sharding import PartitionSpec as P

MESH = pl.DeviceIdType.MESH
SLOPE = 0.01
F32 = jnp.float32
BF16 = jnp.bfloat16
NT = (((1,), (1,)), ((), ()))


def factor(mask):
    return jnp.where(mask == 1, 1.0, SLOPE).astype(F32)


def shift(values, amount):
    return pltpu.roll(values, amount % 128, 1) if amount else values


def beside(ref, planes, row, count):
    sides = []
    for side in range(count):
        blocks = []
        for plane in planes:
            block = ref[plane, pl.ds(row + side, 3)]
            blocks.append(block.reshape(block.shape[0] * block.shape[1], block.shape[2]))
        sides.append(jnp.concatenate(blocks, axis=0) if len(blocks) > 1 else blocks[0])
    return jnp.concatenate(sides, axis=1)


def kernel(
    nx, ny, scale,
    cot_in, mask1_in, mask2_in, field_in, first_in, second_in, bias_in,
    grad_out, first_out, second_out,
    cot_raw, mask1, mask2, field_raw, first_raw, second_raw, bias_raw,
    pad_cot, factors, pad_field, hid3, grad, hidden_grad, acc2, acc1,
    form1, form2, form2_far, form3, turn2, turn3, bias,
    part, part_x, got_x, got_y, got_c, mine, got_pair, both, got_gx, row_sum, got_gy,
    local_sem, f_send, f_recv, p_send, p_recv, o_send, o_recv, pair_sem, s1_send, s1_recv, s2_send, s2_recv,
):
    gx = lax.axis_index("gx")
    core = lax.rem(gx, 2)
    gy = lax.axis_index("gy")

    loads = [
        pltpu.make_async_copy(cot_in, cot_raw, local_sem.at[0]),
        pltpu.make_async_copy(mask2_in, mask2, local_sem.at[1]),
        pltpu.make_async_copy(field_in, field_raw.at[:, 1:3, 16:48], local_sem.at[2]),
        pltpu.make_async_copy(mask1_in, mask1, local_sem.at[3]),
        pltpu.make_async_copy(first_in, first_raw, local_sem.at[4]),
        pltpu.make_async_copy(second_in, second_raw, local_sem.at[5]),
        pltpu.make_async_copy(bias_in, bias_raw, local_sem.at[6]),
    ]
    for load in loads[0:3]:
        load.start()

    left, right = lax.rem(gx + nx - 1, nx), lax.rem(gx + 1, nx)
    down, up = lax.rem(gy + ny - 1, ny), lax.rem(gy + 1, ny)

    barrier = pltpu.get_barrier_semaphore()

    def greet_x(k, _):
        pl.semaphore_signal(barrier, inc=1, device_id=(lax.rem(gx + 2 * k, nx), gy), device_id_type=MESH)
        return 0

    def greet_y(k, _):
        pl.semaphore_signal(barrier, inc=1, device_id=(gx, lax.rem(gy + k, ny)), device_id_type=MESH)
        return 0

    for place in ((left, gy), (right, gy), (left, down), (left, up), (right, down), (right, up)):
        pl.semaphore_signal(barrier, inc=1, device_id=place, device_id_type=MESH)
    lax.fori_loop(1, nx // 2, greet_x, 0)
    lax.fori_loop(1, ny, greet_y, 0)

    loads[0].wait()
    loads[1].wait()
    for load in loads[3:7]:
        load.start()
    for x in range(2):
        for half in range(2):
            rows = slice(16 * half, 16 * half + 16)
            values = cot_raw[:, x, rows, :].astype(F32) * factor(mask2[:, x, rows, :])
            pad_cot[x + 1, 1 + 16 * half : 17 + 16 * half] = jnp.swapaxes(values, 0, 1).astype(BF16)

    loads[2].wait()
    pl.semaphore_wait(barrier, 6 + (nx // 2 - 1) + (ny - 1))

    def remote(src, dst, send, recv, where):
        return pltpu.make_async_remote_copy(
            src_ref=src, dst_ref=dst, send_sem=send, recv_sem=recv, device_id=where, device_id_type=MESH
        )

    places = [(left, gy), (right, gy), (gx, down), (gx, up), (left, down), (left, up), (right, down), (right, up)]
    low, high = slice(16, 32), slice(32, 48)
    inner, before, after = slice(16, 48), slice(0, 16), slice(48, 64)
    field_moves = [
        (field_raw.at[:, 1:2, inner], field_raw.at[:, 3:4, inner]),
        (field_raw.at[:, 2:3, inner], field_raw.at[:, 0:1, inner]),
        (field_raw.at[:, 1:3, low], field_raw.at[:, 1:3, after]),
        (field_raw.at[:, 1:3, high], field_raw.at[:, 1:3, before]),
        (field_raw.at[:, 1:2, low], field_raw.at[:, 3:4, after]),
        (field_raw.at[:, 1:2, high], field_raw.at[:, 3:4, before]),
        (field_raw.at[:, 2:3, low], field_raw.at[:, 0:1, after]),
        (field_raw.at[:, 2:3, high], field_raw.at[:, 0:1, before]),
    ]
    cot_moves = [
        (pad_cot.at[1:2, 1:33], pad_cot.at[3:4, 1:33]),
        (pad_cot.at[2:3, 1:33], pad_cot.at[0:1, 1:33]),
        (pad_cot.at[1:3, 1:2], pad_cot.at[1:3, 33:34]),
        (pad_cot.at[1:3, 32:33], pad_cot.at[1:3, 0:1]),
        (pad_cot.at[1:2, 1:2], pad_cot.at[3:4, 33:34]),
        (pad_cot.at[1:2, 32:33], pad_cot.at[3:4, 0:1]),
        (pad_cot.at[2:3, 1:2], pad_cot.at[0:1, 33:34]),
        (pad_cot.at[2:3, 32:33], pad_cot.at[0:1, 0:1]),
    ]
    field_copies = [
        remote(src, dst, f_send.at[i], f_recv.at[i], places[i]) for i, (src, dst) in enumerate(field_moves)
    ]
    cot_copies = [
        remote(src, dst, p_send.at[i], p_recv.at[i], places[i]) for i, (src, dst) in enumerate(cot_moves)
    ]
    for copy in cot_copies[2:4] + field_copies + cot_copies[0:2] + cot_copies[4:8]:
        copy.start()

    loads[4].wait()
    loads[5].wait()
    loads[6].wait()
    form1[...] = jnp.zeros_like(form1)
    form2[...] = jnp.zeros_like(form2)
    form2_far[...] = jnp.zeros_like(form2_far)
    form3[...] = jnp.zeros_like(form3)
    turn2[...] = jnp.zeros_like(turn2)
    turn3[...] = jnp.zeros_like(turn3)
    for q in range(9):
        dx, dy = q // 3, q % 3
        back2 = 32 * (8 - q)
        back3 = 32 * (3 * dx + 2 - dy)
        for dz in range(3):
            turn2[back2 : back2 + 32, 32 * dz : 32 * dz + 32] = second_raw[3 * q + dz].astype(F32)
        for channel in range(3):
            taps = first_raw[channel].astype(F32)[:, 3 * q : 3 * q + 3]
            form1[0:32, 16 * q + 3 * channel : 16 * q + 3 * channel + 3] = taps
            for dz in range(3):
                turn3[back3 : back3 + 32, 8 * dz + channel : 8 * dz + channel + 1] = taps[:, dz : dz + 1]
    form1[32:64, 48:192] = form1[0:32, 0:144]
    whole2 = jnp.transpose(turn2[...])[0:96].astype(BF16)
    form2[0:96, 0:192] = whole2[:, 96:288]
    form2[96:192, 0:192] = whole2[:, 0:192]
    form2_far[0:96, 0:96] = whole2[:, 0:96]
    form2_far[96:192, 96:192] = whole2[:, 192:288]
    whole3 = jnp.transpose(turn3[...])[0:24]
    for plane in range(4):
        for x in range(2):
            if 0 <= plane - x < 3:
                form3[24 * plane : 24 * plane + 24, 96 * x : 96 * x + 96] = whole3[:, 96 * (plane - x) : 96 * (plane - x) + 96]
    bias[...] = jnp.zeros_like(bias)
    bias[0:8, 0:32] = jnp.broadcast_to(bias_raw[...], (8, 32))
    bias[...] = jnp.broadcast_to(jnp.transpose(bias[0:8])[0:32, 0:1], (32, 128))

    loads[3].wait()
    for x in range(2):
        for half in range(2):
            rows = slice(16 * half, 16 * half + 16)
            factors[x, rows] = jnp.swapaxes(factor(mask1[:, x, rows, :]), 0, 1)

    for x in range(2):
        for rows in (slice(0, 2), slice(34, 36)):
            grad[x, rows] = jnp.zeros((2, 32, 128), BF16)
    mine[...] = jnp.zeros_like(mine)
    for start in (96, 224):
        hid3[:, start : start + 32] = jnp.zeros((4, 32, 1024), BF16)

    def turned(out, x, side):
        total = None
        for tap in range(3):
            start = 96 * x + 32 * tap
            term = shift(out[start : start + 32, 128 * side : 128 * side + 128], tap - 1)
            total = term if total is None else total + term
        return total

    cot_copies[2].wait_recv()
    cot_copies[3].wait_recv()

    def backward_near(i, _):
        out = jnp.dot(form2[...], beside(pad_cot, (1, 2), 8 * i, 8), preferred_element_type=F32)
        for x in range(2):
            for side in range(8):
                hidden_grad[x, 8 * i + side] = turned(out, x, side)
        return 0

    lax.fori_loop(0, 4, backward_near, 0)

    for copy in field_copies:
        copy.wait_recv()

    def spread(plane, _):
        for block in range(4):
            rows = []
            for channel in range(3):
                for dz in range(3):
                    row = field_raw[channel, plane, 16 * block : 16 * block + 16, :].astype(F32)
                    rows.append(shift(row, 1 - dz))
            rows.extend([jnp.zeros((16, 128), F32)] * 7)
            pad_field[plane, 16 * block : 16 * block + 16] = jnp.swapaxes(jnp.stack(rows, axis=0), 0, 1).astype(BF16)
        return 0

    lax.fori_loop(0, 4, spread, 0)
    form1_now = form1[...].astype(BF16)

    def forward(i, _):
        pre = jnp.dot(form1_now, beside(pad_field, range(4), 8 * i + 15, 8), preferred_element_type=F32)
        for x in range(2):
            for side in range(8):
                act = pre[32 * x : 32 * x + 32, 128 * side : 128 * side + 128] + bias[...]
                act = jnp.where(act >= 0, act, SLOPE * act).astype(BF16).astype(F32)
                for tap in range(3):
                    start = 128 * x + 32 * tap
                    hid3[i, start : start + 32, 128 * side : 128 * side + 128] = shift(act, 1 - tap).astype(BF16)
        return 0

    lax.fori_loop(0, 4, forward, 0)

    acc2[...] = jnp.zeros_like(acc2)

    def second_near(i, _):
        rows = beside(pad_cot, (1, 2), 8 * i, 8)
        acc2[0] += lax.dot_general(rows, hid3[i], NT, preferred_element_type=F32)
        return 0

    lax.fori_loop(0, 4, second_near, 0)

    for copy in cot_copies[0:2] + cot_copies[4:8]:
        copy.wait_recv()

    def far(i, _):
        rows = beside(pad_cot, (0, 3), 8 * i, 8)
        acc2[1] += lax.dot_general(rows, hid3[i], NT, preferred_element_type=F32)
        out = jnp.dot(form2_far[...], rows, preferred_element_type=F32)
        for x in range(2):
            for side in range(8):
                total = hidden_grad[x, 8 * i + side] + turned(out, x, side)
                grad[x, 8 * i + side + 2] = (total * factors[x, 8 * i + side]).astype(BF16)
        return 0

    lax.fori_loop(0, 4, far, 0)

    acc1[...] = jnp.zeros_like(acc1)

    def first(i, _):
        rows = beside(pad_field, range(4), 8 * i + 15, 8)
        cells = [
            jnp.concatenate([grad[x, 8 * i + 2 + side] for side in range(8)], axis=1) for x in range(2)
        ]
        acc1[...] += lax.dot_general(jnp.concatenate(cells, axis=0), rows, NT, preferred_element_type=F32)
        return 0

    lax.fori_loop(0, 4, first, 0)
    for q in range(9):
        step, row = (8 - q) // 3, 32 * ((8 - q) % 3)
        terms = []
        for x in range(2):
            plane = step + x
            source, place = ((0, 96 * (plane - 1)) if plane in (1, 2) else (1, 32 * plane))
            terms.append(acc2[source, place + row : place + row + 32, 128 * x : 128 * x + 96])
        mine[:, :, q, 0:96] = (terms[0] + terms[1]).reshape(16, 2, 96)
        term = acc1[0:32, 16 * q : 16 * q + 9] + acc1[32:64, 16 * q + 48 : 16 * q + 57]
        mine[:, :, q, 96:105] = term.reshape(16, 2, 9)

    other = gx + 1 - 2 * core
    pair_copy = remote(mine.at[:, 1 - core], got_pair, pair_sem.at[0], pair_sem.at[1], (other, gy))
    pair_copy.start()
    pair_copy.wait_recv()
    both[...] = mine[:, core] + got_pair[...]

    def row_copy(k):
        to = lax.rem(gx + 2 * k, nx)
        return remote(both.at[to // 2], got_gx.at[k], s1_send.at[k], s1_recv.at[k], (to, gy))

    def send_row(k, _):
        row_copy(k).start()
        return 0

    lax.fori_loop(1, nx // 2, send_row, 0)

    form3_now = form3[...].astype(BF16)

    def scatter_rows(row, count):
        out = jnp.dot(form3_now, beside(grad, range(2), row, count), preferred_element_type=F32)
        for plane in range(4):
            for side in range(count):
                total = None
                for tap in range(3):
                    start = 24 * plane + 8 * tap
                    term = shift(out[start : start + 8, 128 * side : 128 * side + 128], tap - 1)
                    total = term if total is None else total + term
                part[plane, row + side] = total

    def scatter(i, _):
        scatter_rows(8 * i, 8)
        return 0

    lax.fori_loop(0, 4, scatter, 0)
    scatter_rows(32, 2)
    part_x[0] = jnp.swapaxes(part[0, 1:33], 0, 1)[0:3]
    part_x[1] = jnp.swapaxes(part[3, 1:33], 0, 1)[0:3]

    part_moves = [
        (part_x.at[0], got_x.at[1]),
        (part_x.at[1], got_x.at[0]),
        (part.at[1:3, 0], got_y.at[1]),
        (part.at[1:3, 33], got_y.at[0]),
        (part.at[0, 0], got_c.at[3]),
        (part.at[0, 33], got_c.at[2]),
        (part.at[3, 0], got_c.at[1]),
        (part.at[3, 33], got_c.at[0]),
    ]
    part_copies = [
        remote(src, dst, o_send.at[i], o_recv.at[i], places[i]) for i, (src, dst) in enumerate(part_moves)
    ]
    for copy in part_copies:
        copy.start()

    def take_row(k, total):
        row_copy(k).wait_recv()
        return total + got_gx[k]

    row_sum[...] = lax.fori_loop(1, nx // 2, take_row, both[gx // 2])

    def send_sum(k, _):
        to = lax.rem(gy + k, ny)
        remote(row_sum, got_gy.at[k], s2_send.at[k], s2_recv.at[k], (gx, to)).start()
        return 0

    lax.fori_loop(1, ny, send_sum, 0)

    for copy in part_copies:
        copy.wait_recv()
    for x in range(2):
        part[x + 1, 1] += got_y[0, x]
        part[x + 1, 32] += got_y[1, x]
        part[x + 1, 1] += got_c[2 * x]
        part[x + 1, 32] += got_c[2 * x + 1]
    for x in range(2):
        grad_out[:, x] = jnp.swapaxes(part[x + 1, 1:33], 0, 1)[0:3] + got_x[x]

    def sent_row(k, _):
        row_copy(k).wait_send()
        return 0

    for copy in field_copies + cot_copies + part_copies:
        copy.wait_send()
    lax.fori_loop(1, nx // 2, sent_row, 0)
    pair_copy.wait_send()

    def take_sum(k, total):
        to = lax.rem(gy + k, ny)
        remote(row_sum, got_gy.at[k], s2_send.at[k], s2_recv.at[k], (gx, to)).wait_recv()
        return total + got_gy[k]

    total = lax.fori_loop(1, ny, take_sum, row_sum[...]) * scale
    for q in range(9):
        for dz in range(3):
            second_out[3 * q + dz] = total[q : q + 1, 32 * dz : 32 * dz + 32]
        for channel in range(3):
            first_out[channel, :, 3 * q : 3 * q + 3] = total[q : q + 1, 96 + 3 * channel : 96 + 3 * channel + 3]

    def sent_sum(k, _):
        to = lax.rem(gy + k, ny)
        remote(row_sum, got_gy.at[k], s2_send.at[k], s2_recv.at[k], (gx, to)).wait_send()
        return 0

    lax.fori_loop(1, ny, sent_sum, 0)


def put_out(a, b, c, a_out, b_out, c_out):
    a_out[...] = a[...]
    b_out[...] = b[...]
    c_out[...] = c[...]


def on_device(nx, ny, field_in, conv_first, bias_first, conv_second, cotangent, mask_first, mask_second):
    scale = 1.0 / math.sqrt(2 * nx * 32 * ny * 128)
    outside = pl.BlockSpec(memory_space=pltpu.HBM)
    vmem = pl.BlockSpec(memory_space=pltpu.VMEM)
    dma = pltpu.SemaphoreType.DMA
    results = pl.pallas_call(
        functools.partial(kernel, nx, ny, scale),
        out_shape=(
            jax.ShapeDtypeStruct((3, 2, 32, 128), F32),
            jax.ShapeDtypeStruct((3, 1, 27), F32),
            jax.ShapeDtypeStruct((27, 1, 32), F32),
        ),
        in_specs=[outside] * 7,
        out_specs=(vmem, vmem, vmem),
        scratch_shapes=[
            pltpu.VMEM((32, 2, 32, 128), BF16),
            pltpu.VMEM((32, 2, 32, 128), jnp.int32),
            pltpu.VMEM((32, 2, 32, 128), jnp.int32),
            pltpu.VMEM((3, 4, 64, 128), BF16),
            pltpu.VMEM((3, 32, 27), BF16),
            pltpu.VMEM((27, 32, 32), BF16),
            pltpu.VMEM((1, 32), F32),
            pltpu.VMEM((4, 34, 32, 128), BF16),
            pltpu.VMEM((2, 32, 32, 128), F32),
            pltpu.VMEM((4, 64, 16, 128), BF16),
            pltpu.VMEM((4, 256, 1024), BF16),
            pltpu.VMEM((2, 36, 32, 128), BF16),
            pltpu.VMEM((2, 32, 32, 128), F32),
            pltpu.VMEM((2, 192, 256), F32),
            pltpu.VMEM((64, 192), F32),
            pltpu.VMEM((64, 192), F32),
            pltpu.VMEM((192, 192), BF16),
            pltpu.VMEM((192, 192), BF16),
            pltpu.VMEM((96, 192), F32),
            pltpu.VMEM((384, 128), F32),
            pltpu.VMEM((384, 128), F32),
            pltpu.VMEM((32, 128), F32),
            pltpu.VMEM((4, 34, 8, 128), F32),
            pltpu.VMEM((2, 3, 32, 128), F32),
            pltpu.VMEM((2, 3, 32, 128), F32),
            pltpu.VMEM((2, 2, 8, 128), F32),
            pltpu.VMEM((4, 8, 128), F32),
            pltpu.VMEM((16, 2, 9, 128), F32),
            pltpu.VMEM((16, 9, 128), F32),
            pltpu.VMEM((16, 9, 128), F32),
            pltpu.VMEM((nx // 2, 9, 128), F32),
            pltpu.VMEM((9, 128), F32),
            pltpu.VMEM((ny, 9, 128), F32),
            dma((7,)),
            dma((8,)),
            dma((8,)),
            dma((8,)),
            dma((8,)),
            dma((8,)),
            dma((8,)),
            dma((2,)),
            dma((nx // 2,)),
            dma((nx // 2,)),
            dma((ny,)),
            dma((ny,)),
        ],
        compiler_params=pltpu.CompilerParams(
            collective_id=0, has_side_effects=True, vmem_limit_bytes=60 * 1024 * 1024
        ),
    )(
        cotangent, mask_first, mask_second, field_in,
        conv_first.transpose(2, 0, 1), conv_second.transpose(1, 0, 2), bias_first.reshape(1, 32),
    )
    input_grad, grad_first, grad_second = pl.pallas_call(
        put_out,
        out_shape=tuple(jax.ShapeDtypeStruct(r.shape, r.dtype) for r in results),
        in_specs=[vmem] * 3,
        out_specs=(vmem,) * 3,
    )(*results)
    return input_grad, grad_first.transpose(1, 2, 0), grad_second.transpose(1, 0, 2)


def solution(mesh):
    cells = P(None, "gx", "gy", None)
    return jax.shard_map(
        functools.partial(on_device, mesh.shape["gx"], mesh.shape["gy"]),
        mesh=mesh,
        in_specs=(cells, P(), P(), P(), cells, cells, cells),
        out_specs=(cells, P("gx", None, None), P("gx", None, None)),
        check_vma=False,
    )
```

```python
import functools
import math

import jax
import jax.numpy as jnp
from jax import lax
from jax.experimental import pallas as pl
from jax.experimental.pallas import tpu as pltpu
from jax.sharding import PartitionSpec as P

MESH = pl.DeviceIdType.MESH
SLOPE = 0.01
F32 = jnp.float32
BF16 = jnp.bfloat16
NT = (((1,), (1,)), ((), ()))


def factor(mask):
    return jnp.where(mask == 1, 1.0, SLOPE).astype(F32)


def shift(values, amount):
    return pltpu.roll(values, amount % 128, 1) if amount else values


def beside(ref, planes, row, count):
    sides = []
    for side in range(count):
        blocks = []
        for plane in planes:
            block = ref[plane, pl.ds(row + side, 3)]
            blocks.append(block.reshape(block.shape[0] * block.shape[1], block.shape[2]))
        sides.append(jnp.concatenate(blocks, axis=0) if len(blocks) > 1 else blocks[0])
    return jnp.concatenate(sides, axis=1)


def kernel(
    nx, ny, scale,
    cot_in, mask1_in, mask2_in, field_in, first_in, second_in, bias_in,
    grad_out, first_out, second_out,
    cot_raw, mask1, mask2, field_raw, first_raw, second_raw, bias_raw,
    pad_cot, factors, pad_field, hid3, grad, hidden_grad, acc2, acc1,
    form1, form2, form2_far, form3, turn2, turn3, bias,
    part, part_x, got_x, got_y, got_c, mine, got_pair, both, got_z, two_rows, got_xy,
    local_sem, f_send, f_recv, p_send, p_recv, o_send, o_recv, pair_sem, s1_send, s1_recv, s2_send, s2_recv,
):
    gx = lax.axis_index("gx")
    core = lax.rem(gx, 2)
    x_hi = lax.rem(gx // 2, 2)
    nz = nx // 4
    gy = lax.axis_index("gy")

    loads = [
        pltpu.make_async_copy(cot_in, cot_raw, local_sem.at[0]),
        pltpu.make_async_copy(mask2_in, mask2, local_sem.at[1]),
        pltpu.make_async_copy(field_in, field_raw.at[:, 1:3, 16:48], local_sem.at[2]),
        pltpu.make_async_copy(mask1_in, mask1, local_sem.at[3]),
        pltpu.make_async_copy(first_in, first_raw, local_sem.at[4]),
        pltpu.make_async_copy(second_in, second_raw, local_sem.at[5]),
        pltpu.make_async_copy(bias_in, bias_raw, local_sem.at[6]),
    ]
    for load in loads[0:3]:
        load.start()

    left, right = lax.rem(gx + nx - 1, nx), lax.rem(gx + 1, nx)
    down, up = lax.rem(gy + ny - 1, ny), lax.rem(gy + 1, ny)

    barrier = pltpu.get_barrier_semaphore()

    def down_z(k):
        return lax.rem(gx + 4 * k, nx)

    def across(k):
        return gx + 2 * (k // ny) * (1 - 2 * x_hi), lax.rem(gy + lax.rem(k, ny), ny)

    def greet_z(k, _):
        pl.semaphore_signal(barrier, inc=1, device_id=(down_z(k), gy), device_id_type=MESH)
        return 0

    def greet_xy(k, _):
        pl.semaphore_signal(barrier, inc=1, device_id=across(k), device_id_type=MESH)
        return 0

    for place in ((left, gy), (right, gy), (left, down), (left, up), (right, down), (right, up)):
        pl.semaphore_signal(barrier, inc=1, device_id=place, device_id_type=MESH)
    lax.fori_loop(1, 2 * ny, greet_xy, 0)
    lax.fori_loop(1, nz, greet_z, 0)

    loads[0].wait()
    loads[1].wait()
    for load in loads[3:7]:
        load.start()
    for x in range(2):
        for half in range(2):
            rows = slice(16 * half, 16 * half + 16)
            values = cot_raw[:, x, rows, :].astype(F32) * factor(mask2[:, x, rows, :])
            pad_cot[x + 1, 1 + 16 * half : 17 + 16 * half] = jnp.swapaxes(values, 0, 1).astype(BF16)

    loads[2].wait()
    pl.semaphore_wait(barrier, 6 + (nz - 1) + (2 * ny - 1))

    def remote(src, dst, send, recv, where):
        return pltpu.make_async_remote_copy(
            src_ref=src, dst_ref=dst, send_sem=send, recv_sem=recv, device_id=where, device_id_type=MESH
        )

    places = [(left, gy), (right, gy), (gx, down), (gx, up), (left, down), (left, up), (right, down), (right, up)]
    low, high = slice(16, 32), slice(32, 48)
    inner, before, after = slice(16, 48), slice(0, 16), slice(48, 64)
    field_moves = [
        (field_raw.at[:, 1:2, inner], field_raw.at[:, 3:4, inner]),
        (field_raw.at[:, 2:3, inner], field_raw.at[:, 0:1, inner]),
        (field_raw.at[:, 1:3, low], field_raw.at[:, 1:3, after]),
        (field_raw.at[:, 1:3, high], field_raw.at[:, 1:3, before]),
        (field_raw.at[:, 1:2, low], field_raw.at[:, 3:4, after]),
        (field_raw.at[:, 1:2, high], field_raw.at[:, 3:4, before]),
        (field_raw.at[:, 2:3, low], field_raw.at[:, 0:1, after]),
        (field_raw.at[:, 2:3, high], field_raw.at[:, 0:1, before]),
    ]
    cuts = (1, 10, 18, 26, 33)
    chunks = [slice(cuts[i], cuts[i + 1]) for i in range(4)]
    cot_moves = [
        (pad_cot.at[1:3, 1:2], pad_cot.at[1:3, 33:34], places[2]),
        (pad_cot.at[1:3, 32:33], pad_cot.at[1:3, 0:1], places[3]),
        (pad_cot.at[1:2, 1:2], pad_cot.at[3:4, 33:34], places[4]),
        (pad_cot.at[1:2, 32:33], pad_cot.at[3:4, 0:1], places[5]),
        (pad_cot.at[2:3, 1:2], pad_cot.at[0:1, 33:34], places[6]),
        (pad_cot.at[2:3, 32:33], pad_cot.at[0:1, 0:1], places[7]),
    ]
    for chunk in chunks:
        cot_moves.append((pad_cot.at[1:2, chunk], pad_cot.at[3:4, chunk], places[0]))
        cot_moves.append((pad_cot.at[2:3, chunk], pad_cot.at[0:1, chunk], places[1]))
    field_copies = [
        remote(src, dst, f_send.at[i], f_recv.at[i], places[i]) for i, (src, dst) in enumerate(field_moves)
    ]
    cot_copies = [
        remote(src, dst, p_send.at[i], p_recv.at[i], where) for i, (src, dst, where) in enumerate(cot_moves)
    ]
    for copy in cot_copies[0:2] + field_copies + cot_copies[2:14]:
        copy.start()

    loads[4].wait()
    loads[5].wait()
    loads[6].wait()
    form1[...] = jnp.zeros_like(form1)
    form2[...] = jnp.zeros_like(form2)
    form2_far[...] = jnp.zeros_like(form2_far)
    form3[...] = jnp.zeros_like(form3)
    turn2[...] = jnp.zeros_like(turn2)
    turn3[...] = jnp.zeros_like(turn3)
    for q in range(9):
        dx, dy = q // 3, q % 3
        back2 = 32 * (8 - q)
        back3 = 32 * (3 * dx + 2 - dy)
        for dz in range(3):
            turn2[back2 : back2 + 32, 32 * dz : 32 * dz + 32] = second_raw[3 * q + dz].astype(F32)
        for channel in range(3):
            taps = first_raw[channel].astype(F32)[:, 3 * q : 3 * q + 3]
            form1[0:32, 16 * q + 3 * channel : 16 * q + 3 * channel + 3] = taps
            for dz in range(3):
                turn3[back3 : back3 + 32, 8 * dz + channel : 8 * dz + channel + 1] = taps[:, dz : dz + 1]
    form1[32:64, 48:192] = form1[0:32, 0:144]
    whole2 = jnp.transpose(turn2[...])[0:96].astype(BF16)
    form2[0:96, 0:192] = whole2[:, 96:288]
    form2[96:192, 0:192] = whole2[:, 0:192]
    form2_far[0:96, 0:96] = whole2[:, 0:96]
    form2_far[96:192, 96:192] = whole2[:, 192:288]
    whole3 = jnp.transpose(turn3[...])[0:24]
    for plane in range(4):
        for x in range(2):
            if 0 <= plane - x < 3:
                form3[24 * plane : 24 * plane + 24, 96 * x : 96 * x + 96] = whole3[:, 96 * (plane - x) : 96 * (plane - x) + 96]
    bias[...] = jnp.zeros_like(bias)
    bias[0:8, 0:32] = jnp.broadcast_to(bias_raw[...], (8, 32))
    bias[...] = jnp.broadcast_to(jnp.transpose(bias[0:8])[0:32, 0:1], (32, 128))

    loads[3].wait()
    for x in range(2):
        for half in range(2):
            rows = slice(16 * half, 16 * half + 16)
            factors[x, rows] = jnp.swapaxes(factor(mask1[:, x, rows, :]), 0, 1)

    for x in range(2):
        for rows in (slice(0, 2), slice(34, 36)):
            grad[x, rows] = jnp.zeros((2, 32, 128), BF16)
    mine[...] = jnp.zeros_like(mine)
    for start in (96, 224):
        hid3[:, start : start + 32] = jnp.zeros((4, 32, 1024), BF16)

    def turned(out, x, side):
        total = None
        for tap in range(3):
            start = 96 * x + 32 * tap
            term = shift(out[start : start + 32, 128 * side : 128 * side + 128], tap - 1)
            total = term if total is None else total + term
        return total

    cot_copies[0].wait_recv()
    cot_copies[1].wait_recv()

    def backward_near(i, _):
        out = jnp.dot(form2[...], beside(pad_cot, (1, 2), 8 * i, 8), preferred_element_type=F32)
        for x in range(2):
            for side in range(8):
                hidden_grad[x, 8 * i + side] = turned(out, x, side)
        return 0

    lax.fori_loop(0, 4, backward_near, 0)

    def spread(plane, start, count):
        rows = []
        for channel in range(3):
            for dz in range(3):
                row = field_raw[channel, plane, start : start + count, :].astype(F32)
                rows.append(shift(row, 1 - dz))
        rows.extend([jnp.zeros((count, 128), F32)] * 7)
        pad_field[plane, start : start + count] = jnp.swapaxes(jnp.stack(rows, axis=0), 0, 1).astype(BF16)

    for plane in (1, 2):
        spread(plane, 16, 16)
        spread(plane, 32, 16)
    form1_now = form1[...].astype(BF16)
    acc1[...] = jnp.zeros_like(acc1)
    acc2[...] = jnp.zeros_like(acc2)

    for copy in field_copies:
        copy.wait_recv()
    for plane in range(4):
        spread(plane, 8, 8)
        spread(plane, 48, 8)
    for plane in (0, 3):
        spread(plane, 16, 16)
        spread(plane, 32, 16)

    for copy in cot_copies[2:6]:
        copy.wait_recv()
    for i in range(4):
        fields = beside(pad_field, range(4), 8 * i + 15, 8)
        pre = jnp.dot(form1_now, fields, preferred_element_type=F32)
        for x in range(2):
            for side in range(8):
                lanes = slice(128 * side, 128 * side + 128)
                act = pre[32 * x : 32 * x + 32, lanes] + bias[...]
                act = jnp.where(act >= 0, act, SLOPE * act).astype(BF16).astype(F32)
                for tap in range(3):
                    start = 128 * x + 32 * tap
                    hid3[i, start : start + 32, lanes] = shift(act, 1 - tap).astype(BF16)
        for copy in cot_copies[6 + 2 * i : 8 + 2 * i]:
            copy.wait_recv()
        cots = beside(pad_cot, (1, 2, 0, 3), 8 * i, 8)
        out = jnp.dot(form2_far[...], cots[192:384], preferred_element_type=F32)
        for x in range(2):
            for side in range(8):
                total = hidden_grad[x, 8 * i + side] + turned(out, x, side)
                grad[x, 8 * i + side + 2] = (total * factors[x, 8 * i + side]).astype(BF16)
        acc2[...] += lax.dot_general(cots, hid3[i], NT, preferred_element_type=F32)
        cells = [
            jnp.concatenate([grad[x, 8 * i + 2 + side] for side in range(8)], axis=1) for x in range(2)
        ]
        acc1[...] += lax.dot_general(jnp.concatenate(cells, axis=0), fields, NT, preferred_element_type=F32)

    for q in range(9):
        step, row = (8 - q) // 3, 32 * ((8 - q) % 3)
        terms = []
        for x in range(2):
            place = (192, 0, 96, 288)[step + x]
            terms.append(acc2[place + row : place + row + 32, 128 * x : 128 * x + 96])
        mine[:, :, q, 0:96] = (terms[0] + terms[1]).reshape(16, 2, 96)
        term = acc1[0:32, 16 * q : 16 * q + 9] + acc1[32:64, 16 * q + 48 : 16 * q + 57]
        mine[:, :, q, 96:105] = term.reshape(16, 2, 9)

    other = gx + 1 - 2 * core
    pair_copy = remote(mine.at[:, 1 - core], got_pair, pair_sem.at[0], pair_sem.at[1], (other, gy))
    pair_copy.start()
    pair_copy.wait_recv()
    both[...] = mine[:, core] + got_pair[...]

    def z_copy(k):
        to = down_z(k)
        return remote(both.at[pl.ds(2 * (to // 4), 2)], got_z.at[k], s1_send.at[k], s1_recv.at[k], (to, gy))

    def xy_copy(k):
        to = across(k)
        return remote(two_rows.at[lax.rem(to[0] // 2, 2)], got_xy.at[k], s2_send.at[k], s2_recv.at[k], to)

    def send_z(k, _):
        z_copy(k).start()
        return 0

    lax.fori_loop(1, nz, send_z, 0)

    form3_now = form3[...].astype(BF16)

    def scatter_rows(row, count):
        out = jnp.dot(form3_now, beside(grad, range(2), row, count), preferred_element_type=F32)
        for plane in range(4):
            for side in range(count):
                total = None
                for tap in range(3):
                    start = 24 * plane + 8 * tap
                    term = shift(out[start : start + 8, 128 * side : 128 * side + 128], tap - 1)
                    total = term if total is None else total + term
                part[plane, row + side] = total

    def scatter(i, _):
        scatter_rows(8 * i, 8)
        return 0

    lax.fori_loop(0, 4, scatter, 0)
    scatter_rows(32, 2)
    part_x[0] = jnp.swapaxes(part[0, 1:33], 0, 1)[0:3]
    part_x[1] = jnp.swapaxes(part[3, 1:33], 0, 1)[0:3]

    part_moves = [
        (part_x.at[0], got_x.at[1]),
        (part_x.at[1], got_x.at[0]),
        (part.at[1:3, 0], got_y.at[1]),
        (part.at[1:3, 33], got_y.at[0]),
        (part.at[0, 0], got_c.at[3]),
        (part.at[0, 33], got_c.at[2]),
        (part.at[3, 0], got_c.at[1]),
        (part.at[3, 33], got_c.at[0]),
    ]
    part_copies = [
        remote(src, dst, o_send.at[i], o_recv.at[i], places[i]) for i, (src, dst) in enumerate(part_moves)
    ]
    for copy in part_copies:
        copy.start()

    def take_z(k, total):
        z_copy(k).wait_recv()
        return total + got_z[k]

    two_rows[...] = lax.fori_loop(1, nz, take_z, both[pl.ds(2 * (gx // 4), 2)])

    def send_xy(k, _):
        xy_copy(k).start()
        return 0

    lax.fori_loop(1, 2 * ny, send_xy, 0)

    for copy in part_copies:
        copy.wait_recv()
    for x in range(2):
        part[x + 1, 1] += got_y[0, x]
        part[x + 1, 32] += got_y[1, x]
        part[x + 1, 1] += got_c[2 * x]
        part[x + 1, 32] += got_c[2 * x + 1]
    for x in range(2):
        grad_out[:, x] = jnp.swapaxes(part[x + 1, 1:33], 0, 1)[0:3] + got_x[x]

    def sent_z(k, _):
        z_copy(k).wait_send()
        return 0

    for copy in field_copies + cot_copies + part_copies:
        copy.wait_send()
    pair_copy.wait_send()
    lax.fori_loop(1, nz, sent_z, 0)

    def take_xy(k, total):
        xy_copy(k).wait_recv()
        return total + got_xy[k]

    total = lax.fori_loop(1, 2 * ny, take_xy, two_rows[x_hi]) * scale
    for q in range(9):
        for dz in range(3):
            second_out[3 * q + dz] = total[q : q + 1, 32 * dz : 32 * dz + 32]
        for channel in range(3):
            first_out[channel, :, 3 * q : 3 * q + 3] = total[q : q + 1, 96 + 3 * channel : 96 + 3 * channel + 3]

    def sent_xy(k, _):
        xy_copy(k).wait_send()
        return 0

    lax.fori_loop(1, 2 * ny, sent_xy, 0)


def put_out(a, b, c, a_out, b_out, c_out):
    a_out[...] = a[...]
    b_out[...] = b[...]
    c_out[...] = c[...]


def on_device(nx, ny, field_in, conv_first, bias_first, conv_second, cotangent, mask_first, mask_second):
    scale = 1.0 / math.sqrt(2 * nx * 32 * ny * 128)
    outside = pl.BlockSpec(memory_space=pltpu.HBM)
    vmem = pl.BlockSpec(memory_space=pltpu.VMEM)
    dma = pltpu.SemaphoreType.DMA
    results = pl.pallas_call(
        functools.partial(kernel, nx, ny, scale),
        out_shape=(
            jax.ShapeDtypeStruct((3, 2, 32, 128), F32),
            jax.ShapeDtypeStruct((3, 1, 27), F32),
            jax.ShapeDtypeStruct((27, 1, 32), F32),
        ),
        in_specs=[outside] * 7,
        out_specs=(vmem, vmem, vmem),
        scratch_shapes=[
            pltpu.VMEM((32, 2, 32, 128), BF16),
            pltpu.VMEM((32, 2, 32, 128), jnp.int32),
            pltpu.VMEM((32, 2, 32, 128), jnp.int32),
            pltpu.VMEM((3, 4, 64, 128), BF16),
            pltpu.VMEM((3, 32, 27), BF16),
            pltpu.VMEM((27, 32, 32), BF16),
            pltpu.VMEM((1, 32), F32),
            pltpu.VMEM((4, 34, 32, 128), BF16),
            pltpu.VMEM((2, 32, 32, 128), F32),
            pltpu.VMEM((4, 64, 16, 128), BF16),
            pltpu.VMEM((4, 256, 1024), BF16),
            pltpu.VMEM((2, 36, 32, 128), BF16),
            pltpu.VMEM((2, 32, 32, 128), F32),
            pltpu.VMEM((384, 256), F32),
            pltpu.VMEM((64, 192), F32),
            pltpu.VMEM((64, 192), F32),
            pltpu.VMEM((192, 192), BF16),
            pltpu.VMEM((192, 192), BF16),
            pltpu.VMEM((96, 192), F32),
            pltpu.VMEM((384, 128), F32),
            pltpu.VMEM((384, 128), F32),
            pltpu.VMEM((32, 128), F32),
            pltpu.VMEM((4, 34, 8, 128), F32),
            pltpu.VMEM((2, 3, 32, 128), F32),
            pltpu.VMEM((2, 3, 32, 128), F32),
            pltpu.VMEM((2, 2, 8, 128), F32),
            pltpu.VMEM((4, 8, 128), F32),
            pltpu.VMEM((16, 2, 9, 128), F32),
            pltpu.VMEM((16, 9, 128), F32),
            pltpu.VMEM((16, 9, 128), F32),
            pltpu.VMEM((nx // 4, 2, 9, 128), F32),
            pltpu.VMEM((2, 9, 128), F32),
            pltpu.VMEM((2 * ny, 9, 128), F32),
            dma((7,)),
            dma((8,)),
            dma((8,)),
            dma((14,)),
            dma((14,)),
            dma((8,)),
            dma((8,)),
            dma((2,)),
            dma((nx // 4,)),
            dma((nx // 4,)),
            dma((2 * ny,)),
            dma((2 * ny,)),
        ],
        compiler_params=pltpu.CompilerParams(
            collective_id=0, has_side_effects=True, vmem_limit_bytes=60 * 1024 * 1024
        ),
    )(
        cotangent, mask_first, mask_second, field_in,
        conv_first.transpose(2, 0, 1), conv_second.transpose(1, 0, 2), bias_first.reshape(1, 32),
    )
    input_grad, grad_first, grad_second = pl.pallas_call(
        put_out,
        out_shape=tuple(jax.ShapeDtypeStruct(r.shape, r.dtype) for r in results),
        in_specs=[vmem] * 3,
        out_specs=(vmem,) * 3,
    )(*results)
    return input_grad, grad_first.transpose(1, 2, 0), grad_second.transpose(1, 0, 2)


def solution(mesh):
    cells = P(None, "gx", "gy", None)
    return jax.shard_map(
        functools.partial(on_device, mesh.shape["gx"], mesh.shape["gy"]),
        mesh=mesh,
        in_specs=(cells, P(), P(), P(), cells, cells, cells),
        out_specs=(cells, P("gx", None, None), P("gx", None, None)),
        check_vma=False,
    )
```

```python
import functools
import math

import jax
import jax.numpy as jnp
from jax import lax
from jax.experimental import pallas as pl
from jax.experimental.pallas import tpu as pltpu
from jax.sharding import PartitionSpec as P

MESH = pl.DeviceIdType.MESH
SLOPE = 0.01
F32 = jnp.float32
BF16 = jnp.bfloat16
NT = (((1,), (1,)), ((), ()))


def factor(mask):
    return jnp.where(mask == 1, 1.0, SLOPE).astype(F32)


def shift(values, amount):
    return pltpu.roll(values, amount % 128, 1) if amount else values


def beside(ref, planes, row, count):
    sides = []
    for side in range(count):
        blocks = []
        for plane in planes:
            block = ref[plane, pl.ds(row + side, 3)]
            blocks.append(block.reshape(block.shape[0] * block.shape[1], block.shape[2]))
        sides.append(jnp.concatenate(blocks, axis=0) if len(blocks) > 1 else blocks[0])
    return jnp.concatenate(sides, axis=1)


def kernel(
    nx, ny, scale,
    cot_in, mask1_in, mask2_in, field_in, first_in, second_in, bias_in,
    grad_out, first_out, second_out,
    cot_raw, mask1, mask2, field_raw, first_raw, second_raw, bias_raw,
    pad_cot, factors, pad_field, hid3, grad, hidden_grad, acc2, acc1,
    form1, form2, form2_far, form3, turn2, turn3, bias,
    part, part_x, got_x, got_y, got_c, mine, got_pair, both, got_z, two_rows, got_xy,
    local_sem, f_send, f_recv, p_send, p_recv, o_send, o_recv, pair_sem, s1_send, s1_recv, s2_send, s2_recv,
):
    gx = lax.axis_index("gx")
    core = lax.rem(gx, 2)
    x_hi = lax.rem(gx // 2, 2)
    nz = nx // 4
    gy = lax.axis_index("gy")

    loads = [
        pltpu.make_async_copy(cot_in, cot_raw, local_sem.at[0]),
        pltpu.make_async_copy(mask2_in, mask2, local_sem.at[1]),
        pltpu.make_async_copy(field_in, field_raw.at[:, 1:3, 16:48], local_sem.at[2]),
        pltpu.make_async_copy(mask1_in, mask1, local_sem.at[3]),
        pltpu.make_async_copy(first_in, first_raw, local_sem.at[4]),
        pltpu.make_async_copy(second_in, second_raw, local_sem.at[5]),
        pltpu.make_async_copy(bias_in, bias_raw, local_sem.at[6]),
    ]
    for load in loads[0:3]:
        load.start()

    left, right = lax.rem(gx + nx - 1, nx), lax.rem(gx + 1, nx)
    down, up = lax.rem(gy + ny - 1, ny), lax.rem(gy + 1, ny)

    barrier = pltpu.get_barrier_semaphore()

    def down_z(k):
        return lax.rem(gx + 4 * k, nx)

    def across(k):
        return gx + 2 * (k // ny) * (1 - 2 * x_hi), lax.rem(gy + lax.rem(k, ny), ny)

    def greet_z(k, _):
        pl.semaphore_signal(barrier, inc=1, device_id=(down_z(k), gy), device_id_type=MESH)
        return 0

    def greet_xy(k, _):
        pl.semaphore_signal(barrier, inc=1, device_id=across(k), device_id_type=MESH)
        return 0

    for place in ((left, gy), (right, gy), (left, down), (left, up), (right, down), (right, up)):
        pl.semaphore_signal(barrier, inc=1, device_id=place, device_id_type=MESH)
    lax.fori_loop(1, 2 * ny, greet_xy, 0)
    lax.fori_loop(1, nz, greet_z, 0)

    loads[0].wait()
    loads[1].wait()
    for load in loads[3:7]:
        load.start()
    for x in range(2):
        for half in range(2):
            rows = slice(16 * half, 16 * half + 16)
            values = cot_raw[:, x, rows, :].astype(F32) * factor(mask2[:, x, rows, :])
            pad_cot[x + 1, 1 + 16 * half : 17 + 16 * half] = jnp.swapaxes(values, 0, 1).astype(BF16)

    loads[2].wait()
    pl.semaphore_wait(barrier, 6 + (nz - 1) + (2 * ny - 1))

    def remote(src, dst, send, recv, where):
        return pltpu.make_async_remote_copy(
            src_ref=src, dst_ref=dst, send_sem=send, recv_sem=recv, device_id=where, device_id_type=MESH
        )

    places = [(left, gy), (right, gy), (gx, down), (gx, up), (left, down), (left, up), (right, down), (right, up)]
    low, high = slice(16, 32), slice(32, 48)
    inner, before, after = slice(16, 48), slice(0, 16), slice(48, 64)
    field_moves = [
        (field_raw.at[:, 1:2, inner], field_raw.at[:, 3:4, inner]),
        (field_raw.at[:, 2:3, inner], field_raw.at[:, 0:1, inner]),
        (field_raw.at[:, 1:3, low], field_raw.at[:, 1:3, after]),
        (field_raw.at[:, 1:3, high], field_raw.at[:, 1:3, before]),
        (field_raw.at[:, 1:2, low], field_raw.at[:, 3:4, after]),
        (field_raw.at[:, 1:2, high], field_raw.at[:, 3:4, before]),
        (field_raw.at[:, 2:3, low], field_raw.at[:, 0:1, after]),
        (field_raw.at[:, 2:3, high], field_raw.at[:, 0:1, before]),
    ]
    cuts = (1, 10, 18, 26, 33)
    chunks = [slice(cuts[i], cuts[i + 1]) for i in range(4)]
    cot_moves = [
        (pad_cot.at[1:3, 1:2], pad_cot.at[1:3, 33:34], places[2]),
        (pad_cot.at[1:3, 32:33], pad_cot.at[1:3, 0:1], places[3]),
        (pad_cot.at[1:2, 1:2], pad_cot.at[3:4, 33:34], places[4]),
        (pad_cot.at[1:2, 32:33], pad_cot.at[3:4, 0:1], places[5]),
        (pad_cot.at[2:3, 1:2], pad_cot.at[0:1, 33:34], places[6]),
        (pad_cot.at[2:3, 32:33], pad_cot.at[0:1, 0:1], places[7]),
    ]
    for chunk in chunks:
        cot_moves.append((pad_cot.at[1:2, chunk], pad_cot.at[3:4, chunk], places[0]))
        cot_moves.append((pad_cot.at[2:3, chunk], pad_cot.at[0:1, chunk], places[1]))
    field_copies = [
        remote(src, dst, f_send.at[i], f_recv.at[i], places[i]) for i, (src, dst) in enumerate(field_moves)
    ]
    cot_copies = [
        remote(src, dst, p_send.at[i], p_recv.at[i], where) for i, (src, dst, where) in enumerate(cot_moves)
    ]
    for copy in cot_copies[0:2] + field_copies + cot_copies[2:14]:
        copy.start()

    loads[4].wait()
    loads[5].wait()
    loads[6].wait()
    form1[...] = jnp.zeros_like(form1)
    form2[...] = jnp.zeros_like(form2)
    form2_far[...] = jnp.zeros_like(form2_far)
    form3[...] = jnp.zeros_like(form3)
    turn2[...] = jnp.zeros_like(turn2)
    turn3[...] = jnp.zeros_like(turn3)
    for q in range(9):
        dx, dy = q // 3, q % 3
        back2 = 32 * (8 - q)
        back3 = 32 * (3 * dx + 2 - dy)
        for dz in range(3):
            turn2[back2 : back2 + 32, 32 * dz : 32 * dz + 32] = second_raw[3 * q + dz].astype(F32)
        for channel in range(3):
            taps = first_raw[channel].astype(F32)[:, 3 * q : 3 * q + 3]
            form1[0:32, 16 * q + 3 * channel : 16 * q + 3 * channel + 3] = taps
            for dz in range(3):
                turn3[back3 : back3 + 32, 8 * dz + channel : 8 * dz + channel + 1] = taps[:, dz : dz + 1]
    form1[32:64, 48:192] = form1[0:32, 0:144]
    whole2 = jnp.transpose(turn2[...])[0:96].astype(BF16)
    form2[0:96, 0:192] = whole2[:, 96:288]
    form2[96:192, 0:192] = whole2[:, 0:192]
    form2_far[0:96, 0:96] = whole2[:, 0:96]
    form2_far[96:192, 96:192] = whole2[:, 192:288]
    whole3 = jnp.transpose(turn3[...])[0:24]
    for plane in range(4):
        for x in range(2):
            if 0 <= plane - x < 3:
                form3[24 * plane : 24 * plane + 24, 96 * x : 96 * x + 96] = whole3[:, 96 * (plane - x) : 96 * (plane - x) + 96]
    bias[...] = jnp.zeros_like(bias)
    bias[0:8, 0:32] = jnp.broadcast_to(bias_raw[...], (8, 32))
    bias[...] = jnp.broadcast_to(jnp.transpose(bias[0:8])[0:32, 0:1], (32, 128))

    loads[3].wait()
    for x in range(2):
        for half in range(2):
            rows = slice(16 * half, 16 * half + 16)
            factors[x, rows] = jnp.swapaxes(factor(mask1[:, x, rows, :]), 0, 1)

    for x in range(2):
        for rows in (slice(0, 2), slice(34, 36)):
            grad[x, rows] = jnp.zeros((2, 32, 128), BF16)
    for start in (96, 224):
        hid3[:, start : start + 32] = jnp.zeros((4, 32, 1024), BF16)

    def turned(out, x, side):
        total = None
        for tap in range(3):
            start = 96 * x + 32 * tap
            term = shift(out[start : start + 32, 128 * side : 128 * side + 128], tap - 1)
            total = term if total is None else total + term
        return total

    cot_copies[0].wait_recv()
    cot_copies[1].wait_recv()

    def backward_near(i, _):
        out = jnp.dot(form2[...], beside(pad_cot, (1, 2), 8 * i, 8), preferred_element_type=F32)
        for x in range(2):
            for side in range(8):
                hidden_grad[x, 8 * i + side] = turned(out, x, side)
        return 0

    lax.fori_loop(0, 4, backward_near, 0)

    def spread(plane, start, count):
        rows = []
        for channel in range(3):
            for dz in range(3):
                row = field_raw[channel, plane, start : start + count, :].astype(F32)
                rows.append(shift(row, 1 - dz))
        rows.extend([jnp.zeros((count, 128), F32)] * 7)
        pad_field[plane, start : start + count] = jnp.swapaxes(jnp.stack(rows, axis=0), 0, 1).astype(BF16)

    for plane in (1, 2):
        spread(plane, 16, 16)
        spread(plane, 32, 16)
    form1_now = form1[...].astype(BF16)
    acc1[...] = jnp.zeros_like(acc1)
    acc2[...] = jnp.zeros_like(acc2)

    for copy in field_copies:
        copy.wait_recv()
    for plane in range(4):
        spread(plane, 8, 8)
        spread(plane, 48, 8)
    for plane in (0, 3):
        spread(plane, 16, 16)
        spread(plane, 32, 16)

    for copy in cot_copies[2:6]:
        copy.wait_recv()
    for i in range(4):
        fields = beside(pad_field, range(4), 8 * i + 15, 8)
        pre = jnp.dot(form1_now, fields, preferred_element_type=F32)
        for x in range(2):
            for side in range(8):
                lanes = slice(128 * side, 128 * side + 128)
                act = pre[32 * x : 32 * x + 32, lanes] + bias[...]
                act = jnp.where(act >= 0, act, SLOPE * act).astype(BF16).astype(F32)
                for tap in range(3):
                    start = 128 * x + 32 * tap
                    hid3[i, start : start + 32, lanes] = shift(act, 1 - tap).astype(BF16)
        for copy in cot_copies[6 + 2 * i : 8 + 2 * i]:
            copy.wait_recv()
        cots = beside(pad_cot, (1, 2, 0, 3), 8 * i, 8)
        out = jnp.dot(form2_far[...], cots[192:384], preferred_element_type=F32)
        for x in range(2):
            for side in range(8):
                total = hidden_grad[x, 8 * i + side] + turned(out, x, side)
                grad[x, 8 * i + side + 2] = (total * factors[x, 8 * i + side]).astype(BF16)
        acc2[...] += lax.dot_general(cots, hid3[i], NT, preferred_element_type=F32)
        cells = [
            jnp.concatenate([grad[x, 8 * i + 2 + side] for side in range(8)], axis=1) for x in range(2)
        ]
        acc1[:, 0:192] += lax.dot_general(jnp.concatenate(cells, axis=0), fields, NT, preferred_element_type=F32)

    rows = []
    for q in range(9):
        step, row = (8 - q) // 3, 32 * ((8 - q) % 3)
        terms = []
        for x in range(2):
            place = (192, 0, 96, 288)[step + x]
            terms.append(acc2[place + row : place + row + 32, 128 * x : 128 * x + 128])
        rows.append(terms[0] + terms[1])
    rows.append(acc1[0:32, 0:128] + acc1[32:64, 48:176])
    acc1[0:32, 128:144] += acc1[32:64, 176:192]
    rows.append(acc1[0:32, 128:256])
    rows.extend([jnp.zeros((32, 128), F32)] * 5)
    mine[...] = jnp.swapaxes(jnp.stack(rows, axis=0), 0, 1).reshape(16, 2, 16, 128)

    other = gx + 1 - 2 * core
    pair_copy = remote(mine.at[:, 1 - core, 0:11], got_pair, pair_sem.at[0], pair_sem.at[1], (other, gy))
    pair_copy.start()
    pair_copy.wait_recv()
    both[...] = mine[:, core, 0:11] + got_pair[...]

    def z_copy(k):
        to = down_z(k)
        return remote(both.at[pl.ds(2 * (to // 4), 2)], got_z.at[k], s1_send.at[k], s1_recv.at[k], (to, gy))

    def xy_copy(k):
        to = across(k)
        return remote(two_rows.at[lax.rem(to[0] // 2, 2)], got_xy.at[k], s2_send.at[k], s2_recv.at[k], to)

    def send_z(k, _):
        z_copy(k).start()
        return 0

    lax.fori_loop(1, nz, send_z, 0)

    form3_now = form3[...].astype(BF16)

    def scatter_rows(row, count):
        out = jnp.dot(form3_now, beside(grad, range(2), row, count), preferred_element_type=F32)
        for plane in range(4):
            for side in range(count):
                total = None
                for tap in range(3):
                    start = 24 * plane + 8 * tap
                    term = shift(out[start : start + 8, 128 * side : 128 * side + 128], tap - 1)
                    total = term if total is None else total + term
                part[plane, row + side] = total

    def scatter(i, _):
        scatter_rows(8 * i, 8)
        return 0

    lax.fori_loop(0, 4, scatter, 0)
    scatter_rows(32, 2)
    part_x[0] = jnp.swapaxes(part[0, 1:33], 0, 1)[0:3]
    part_x[1] = jnp.swapaxes(part[3, 1:33], 0, 1)[0:3]

    part_moves = [
        (part_x.at[0], got_x.at[1]),
        (part_x.at[1], got_x.at[0]),
        (part.at[1:3, 0], got_y.at[1]),
        (part.at[1:3, 33], got_y.at[0]),
        (part.at[0, 0], got_c.at[3]),
        (part.at[0, 33], got_c.at[2]),
        (part.at[3, 0], got_c.at[1]),
        (part.at[3, 33], got_c.at[0]),
    ]
    part_copies = [
        remote(src, dst, o_send.at[i], o_recv.at[i], places[i]) for i, (src, dst) in enumerate(part_moves)
    ]
    for copy in part_copies:
        copy.start()

    def take_z(k, total):
        z_copy(k).wait_recv()
        return total + got_z[k]

    two_rows[...] = lax.fori_loop(1, nz, take_z, both[pl.ds(2 * (gx // 4), 2)])

    def send_xy(k, _):
        xy_copy(k).start()
        return 0

    lax.fori_loop(1, 2 * ny, send_xy, 0)

    for copy in part_copies:
        copy.wait_recv()
    for x in range(2):
        part[x + 1, 1] += got_y[0, x]
        part[x + 1, 32] += got_y[1, x]
        part[x + 1, 1] += got_c[2 * x]
        part[x + 1, 32] += got_c[2 * x + 1]
    for x in range(2):
        grad_out[:, x] = jnp.swapaxes(part[x + 1, 1:33], 0, 1)[0:3] + got_x[x]

    def sent_z(k, _):
        z_copy(k).wait_send()
        return 0

    for copy in field_copies + cot_copies + part_copies:
        copy.wait_send()
    pair_copy.wait_send()
    lax.fori_loop(1, nz, sent_z, 0)

    def take_xy(k, total):
        xy_copy(k).wait_recv()
        return total + got_xy[k]

    total = lax.fori_loop(1, 2 * ny, take_xy, two_rows[x_hi]) * scale
    for q in range(9):
        for dz in range(3):
            second_out[3 * q + dz] = total[q : q + 1, 32 * dz : 32 * dz + 32]
        for channel in range(3):
            row, lane = 9 + q // 8, 16 * (q % 8) + 3 * channel
            first_out[channel, :, 3 * q : 3 * q + 3] = total[row : row + 1, lane : lane + 3]

    def sent_xy(k, _):
        xy_copy(k).wait_send()
        return 0

    lax.fori_loop(1, 2 * ny, sent_xy, 0)


def put_out(a, b, c, a_out, b_out, c_out):
    a_out[...] = a[...]
    b_out[...] = b[...]
    c_out[...] = c[...]


def on_device(nx, ny, field_in, conv_first, bias_first, conv_second, cotangent, mask_first, mask_second):
    scale = 1.0 / math.sqrt(2 * nx * 32 * ny * 128)
    outside = pl.BlockSpec(memory_space=pltpu.HBM)
    vmem = pl.BlockSpec(memory_space=pltpu.VMEM)
    dma = pltpu.SemaphoreType.DMA
    results = pl.pallas_call(
        functools.partial(kernel, nx, ny, scale),
        out_shape=(
            jax.ShapeDtypeStruct((3, 2, 32, 128), F32),
            jax.ShapeDtypeStruct((3, 1, 27), F32),
            jax.ShapeDtypeStruct((27, 1, 32), F32),
        ),
        in_specs=[outside] * 7,
        out_specs=(vmem, vmem, vmem),
        scratch_shapes=[
            pltpu.VMEM((32, 2, 32, 128), BF16),
            pltpu.VMEM((32, 2, 32, 128), jnp.int32),
            pltpu.VMEM((32, 2, 32, 128), jnp.int32),
            pltpu.VMEM((3, 4, 64, 128), BF16),
            pltpu.VMEM((3, 32, 27), BF16),
            pltpu.VMEM((27, 32, 32), BF16),
            pltpu.VMEM((1, 32), F32),
            pltpu.VMEM((4, 34, 32, 128), BF16),
            pltpu.VMEM((2, 32, 32, 128), F32),
            pltpu.VMEM((4, 64, 16, 128), BF16),
            pltpu.VMEM((4, 256, 1024), BF16),
            pltpu.VMEM((2, 36, 32, 128), BF16),
            pltpu.VMEM((2, 32, 32, 128), F32),
            pltpu.VMEM((384, 256), F32),
            pltpu.VMEM((64, 256), F32),
            pltpu.VMEM((64, 192), F32),
            pltpu.VMEM((192, 192), BF16),
            pltpu.VMEM((192, 192), BF16),
            pltpu.VMEM((96, 192), F32),
            pltpu.VMEM((384, 128), F32),
            pltpu.VMEM((384, 128), F32),
            pltpu.VMEM((32, 128), F32),
            pltpu.VMEM((4, 34, 8, 128), F32),
            pltpu.VMEM((2, 3, 32, 128), F32),
            pltpu.VMEM((2, 3, 32, 128), F32),
            pltpu.VMEM((2, 2, 8, 128), F32),
            pltpu.VMEM((4, 8, 128), F32),
            pltpu.VMEM((16, 2, 16, 128), F32),
            pltpu.VMEM((16, 11, 128), F32),
            pltpu.VMEM((16, 11, 128), F32),
            pltpu.VMEM((nx // 4, 2, 11, 128), F32),
            pltpu.VMEM((2, 11, 128), F32),
            pltpu.VMEM((2 * ny, 11, 128), F32),
            dma((7,)),
            dma((8,)),
            dma((8,)),
            dma((14,)),
            dma((14,)),
            dma((8,)),
            dma((8,)),
            dma((2,)),
            dma((nx // 4,)),
            dma((nx // 4,)),
            dma((2 * ny,)),
            dma((2 * ny,)),
        ],
        compiler_params=pltpu.CompilerParams(
            collective_id=0, has_side_effects=True, vmem_limit_bytes=40 * 1024 * 1024
        ),
    )(*[pltpu.with_memory_space_constraint(a, pltpu.HBM) for a in (
        cotangent, mask_first, mask_second, field_in,
        conv_first.transpose(2, 0, 1), conv_second.transpose(1, 0, 2), bias_first.reshape(1, 32),
    )])
    results = [pltpu.with_memory_space_constraint(r, pltpu.VMEM) for r in results]
    input_grad, grad_first, grad_second = pl.pallas_call(
        put_out,
        out_shape=tuple(jax.ShapeDtypeStruct(r.shape, r.dtype) for r in results),
        in_specs=[vmem] * 3,
        out_specs=(vmem,) * 3,

    )(*results)
    return input_grad, grad_first.transpose(1, 2, 0), grad_second.transpose(1, 0, 2)


def solution(mesh):
    cells = P(None, "gx", "gy", None)
    return jax.shard_map(
        functools.partial(on_device, mesh.shape["gx"], mesh.shape["gy"]),
        mesh=mesh,
        in_specs=(cells, P(), P(), P(), cells, cells, cells),
        out_specs=(cells, P("gx", None, None), P("gx", None, None)),
        check_vma=False,
    )
```

```python
import functools
import math

import jax
import jax.numpy as jnp
from jax import lax
from jax.experimental import pallas as pl
from jax.experimental.pallas import tpu as pltpu
from jax.sharding import PartitionSpec as P

MESH = pl.DeviceIdType.MESH
SLOPE = 0.01
F32 = jnp.float32
BF16 = jnp.bfloat16
NT = (((1,), (1,)), ((), ()))


def factor(mask):
    return jnp.where(mask == 1, 1.0, SLOPE).astype(F32)


def shift(values, amount):
    return pltpu.roll(values, amount % 128, 1) if amount else values


def beside(ref, planes, row, count):
    sides = []
    for side in range(count):
        blocks = []
        for plane in planes:
            block = ref[plane, pl.ds(row + side, 3)]
            blocks.append(block.reshape(block.shape[0] * block.shape[1], block.shape[2]))
        sides.append(jnp.concatenate(blocks, axis=0) if len(blocks) > 1 else blocks[0])
    return jnp.concatenate(sides, axis=1)


def kernel(
    nx, ny, scale,
    cot_in, mask1_in, mask2_in, field_in, first_in, second_in, bias_in,
    grad_out, first_out, second_out,
    cot_raw, mask1, mask2, field_raw, first_raw, second_raw, bias_raw,
    pad_cot, factors, pad_field, hid3, grad, hidden_grad, acc2, acc1,
    form1, form2, form2_far, form3, turn2, turn3, bias,
    part, part_x, got_x, got_y, got_c, mine, got_pair, both, got_z, two_rows, got_xy,
    local_sem, f_send, f_recv, p_send, p_recv, o_send, o_recv, pair_sem, s1_send, s1_recv, s2_send, s2_recv,
):
    gx = lax.axis_index("gx")
    core = lax.rem(gx, 2)
    x_hi = lax.rem(gx // 2, 2)
    nz = nx // 4
    gy = lax.axis_index("gy")

    loads = [
        pltpu.make_async_copy(cot_in, cot_raw, local_sem.at[0]),
        pltpu.make_async_copy(mask2_in, mask2, local_sem.at[1]),
        pltpu.make_async_copy(field_in, field_raw.at[:, 1:3, 16:48], local_sem.at[2]),
        pltpu.make_async_copy(mask1_in, mask1, local_sem.at[3]),
        pltpu.make_async_copy(first_in, first_raw, local_sem.at[4]),
        pltpu.make_async_copy(second_in, second_raw, local_sem.at[5]),
        pltpu.make_async_copy(bias_in, bias_raw, local_sem.at[6]),
    ]

    left, right = lax.rem(gx + nx - 1, nx), lax.rem(gx + 1, nx)
    down, up = lax.rem(gy + ny - 1, ny), lax.rem(gy + 1, ny)

    barrier = pltpu.get_barrier_semaphore()

    def down_z(k):
        return lax.rem(gx + 4 * k, nx)

    def across(k):
        return gx + 2 * (k // ny) * (1 - 2 * x_hi), lax.rem(gy + lax.rem(k, ny), ny)

    def greet_z(k, _):
        far = lax.rem(k + nz // 2 - 2, nz - 1) + 1
        pl.semaphore_signal(barrier, inc=1, device_id=(down_z(far), gy), device_id_type=MESH)
        return 0

    lax.fori_loop(1, nz, greet_z, 0)

    def greet_xy(k, _):
        pl.semaphore_signal(barrier, inc=1, device_id=across(2 * ny - k), device_id_type=MESH)
        return 0

    lax.fori_loop(1, 2 * ny, greet_xy, 0)

    for place in ((left, gy), (right, gy), (left, down), (left, up), (right, down), (right, up)):
        pl.semaphore_signal(barrier, inc=1, device_id=place, device_id_type=MESH)

    for load in loads[0:3]:
        load.start()

    loads[0].wait()
    loads[1].wait()
    for load in loads[3:7]:
        load.start()
    for x in range(2):
        for half in range(2):
            rows = slice(16 * half, 16 * half + 16)
            values = cot_raw[:, x, rows, :].astype(F32) * factor(mask2[:, x, rows, :])
            pad_cot[x + 1, 1 + 16 * half : 17 + 16 * half] = jnp.swapaxes(values, 0, 1).astype(BF16)

    loads[2].wait()
    def spread(plane, start, count):
        rows = []
        for channel in range(3):
            for dz in range(3):
                row = field_raw[channel, plane, start : start + count, :].astype(F32)
                rows.append(shift(row, 1 - dz))
        rows.extend([jnp.zeros((count, 128), F32)] * 7)
        pad_field[plane, start : start + count] = jnp.swapaxes(jnp.stack(rows, axis=0), 0, 1).astype(BF16)

    for plane in (1, 2):
        spread(plane, 16, 16)
        spread(plane, 32, 16)
    pl.semaphore_wait(barrier, 6 + (nz - 1) + (2 * ny - 1))

    def remote(src, dst, send, recv, where):
        return pltpu.make_async_remote_copy(
            src_ref=src, dst_ref=dst, send_sem=send, recv_sem=recv, device_id=where, device_id_type=MESH
        )

    places = [(left, gy), (right, gy), (gx, down), (gx, up), (left, down), (left, up), (right, down), (right, up)]
    inner = slice(16, 48)
    field_moves = [
        (field_raw.at[:, 1:2, inner], field_raw.at[:, 3:4, inner]),
        (field_raw.at[:, 2:3, inner], field_raw.at[:, 0:1, inner]),
        (pad_field.at[1:3, 16:17], pad_field.at[1:3, 48:49]),
        (pad_field.at[1:3, 47:48], pad_field.at[1:3, 15:16]),
        (pad_field.at[1:2, 16:17], pad_field.at[3:4, 48:49]),
        (pad_field.at[1:2, 47:48], pad_field.at[3:4, 15:16]),
        (pad_field.at[2:3, 16:17], pad_field.at[0:1, 48:49]),
        (pad_field.at[2:3, 47:48], pad_field.at[0:1, 15:16]),
    ]
    cuts = (1, 10, 18, 26, 33)
    chunks = [slice(cuts[i], cuts[i + 1]) for i in range(4)]
    cot_moves = [
        (pad_cot.at[1:3, 1:2], pad_cot.at[1:3, 33:34], places[2]),
        (pad_cot.at[1:3, 32:33], pad_cot.at[1:3, 0:1], places[3]),
        (pad_cot.at[1:2, 1:2], pad_cot.at[3:4, 33:34], places[4]),
        (pad_cot.at[1:2, 32:33], pad_cot.at[3:4, 0:1], places[5]),
        (pad_cot.at[2:3, 1:2], pad_cot.at[0:1, 33:34], places[6]),
        (pad_cot.at[2:3, 32:33], pad_cot.at[0:1, 0:1], places[7]),
    ]
    for chunk in chunks:
        cot_moves.append((pad_cot.at[1:2, chunk], pad_cot.at[3:4, chunk], places[0]))
        cot_moves.append((pad_cot.at[2:3, chunk], pad_cot.at[0:1, chunk], places[1]))
    field_copies = [
        remote(src, dst, f_send.at[i], f_recv.at[i], places[i]) for i, (src, dst) in enumerate(field_moves)
    ]
    cot_copies = [
        remote(src, dst, p_send.at[i], p_recv.at[i], where) for i, (src, dst, where) in enumerate(cot_moves)
    ]
    for copy in cot_copies[0:2] + field_copies + cot_copies[2:14]:
        copy.start()

    loads[4].wait()
    loads[5].wait()
    loads[6].wait()
    form1[...] = jnp.zeros_like(form1)
    form2[...] = jnp.zeros_like(form2)
    form2_far[...] = jnp.zeros_like(form2_far)
    form3[...] = jnp.zeros_like(form3)
    turn2[...] = jnp.zeros_like(turn2)
    turn3[...] = jnp.zeros_like(turn3)
    for q in range(9):
        dx, dy = q // 3, q % 3
        back2 = 32 * (8 - q)
        back3 = 32 * (3 * dx + 2 - dy)
        for dz in range(3):
            turn2[back2 : back2 + 32, 32 * dz : 32 * dz + 32] = second_raw[3 * q + dz].astype(F32)
        for channel in range(3):
            taps = first_raw[channel].astype(F32)[:, 3 * q : 3 * q + 3]
            form1[0:32, 16 * q + 3 * channel : 16 * q + 3 * channel + 3] = taps
            for dz in range(3):
                turn3[back3 : back3 + 32, 8 * dz + channel : 8 * dz + channel + 1] = taps[:, dz : dz + 1]
    form1[32:64, 48:192] = form1[0:32, 0:144]
    whole2 = jnp.transpose(turn2[...])[0:96].astype(BF16)
    form2[0:96, 0:192] = whole2[:, 96:288]
    form2[96:192, 0:192] = whole2[:, 0:192]
    form2_far[0:96, 0:96] = whole2[:, 0:96]
    form2_far[96:192, 96:192] = whole2[:, 192:288]
    whole3 = jnp.transpose(turn3[...])[0:24]
    for plane in range(4):
        for x in range(2):
            if 0 <= plane - x < 3:
                form3[24 * plane : 24 * plane + 24, 96 * x : 96 * x + 96] = whole3[:, 96 * (plane - x) : 96 * (plane - x) + 96]
    bias[...] = jnp.zeros_like(bias)
    bias[0:8, 0:32] = jnp.broadcast_to(bias_raw[...], (8, 32))
    bias[...] = jnp.broadcast_to(jnp.transpose(bias[0:8])[0:32, 0:1], (32, 128))

    loads[3].wait()
    for x in range(2):
        for half in range(2):
            rows = slice(16 * half, 16 * half + 16)
            factors[x, rows] = jnp.swapaxes(factor(mask1[:, x, rows, :]), 0, 1)

    for x in range(2):
        for rows in (slice(0, 2), slice(34, 36)):
            grad[x, rows] = jnp.zeros((2, 32, 128), BF16)
    for start in (96, 224):
        hid3[:, start : start + 32] = jnp.zeros((4, 32, 1024), BF16)

    def turned(out, x, side):
        total = None
        for tap in range(3):
            start = 96 * x + 32 * tap
            term = shift(out[start : start + 32, 128 * side : 128 * side + 128], tap - 1)
            total = term if total is None else total + term
        return total

    cot_copies[0].wait_recv()
    cot_copies[1].wait_recv()

    def backward_near(i, _):
        out = jnp.dot(form2[...], beside(pad_cot, (1, 2), 8 * i, 8), preferred_element_type=F32)
        for x in range(2):
            for side in range(8):
                hidden_grad[x, 8 * i + side] = turned(out, x, side)
        return 0

    lax.fori_loop(0, 4, backward_near, 0)

    form1_now = form1[...].astype(BF16)
    acc1[...] = jnp.zeros_like(acc1)
    acc2[...] = jnp.zeros_like(acc2)

    for copy in field_copies:
        copy.wait_recv()
    for plane in (0, 3):
        spread(plane, 16, 16)
        spread(plane, 32, 16)

    for copy in cot_copies[2:6]:
        copy.wait_recv()
    for i in range(4):
        fields = beside(pad_field, range(4), 8 * i + 15, 8)
        pre = jnp.dot(form1_now, fields, preferred_element_type=F32)
        for x in range(2):
            for side in range(8):
                lanes = slice(128 * side, 128 * side + 128)
                act = pre[32 * x : 32 * x + 32, lanes] + bias[...]
                act = jnp.where(act >= 0, act, SLOPE * act).astype(BF16).astype(F32)
                for tap in range(3):
                    start = 128 * x + 32 * tap
                    hid3[i, start : start + 32, lanes] = shift(act, 1 - tap).astype(BF16)
        for copy in cot_copies[6 + 2 * i : 8 + 2 * i]:
            copy.wait_recv()
        cots = beside(pad_cot, (1, 2, 0, 3), 8 * i, 8)
        out = jnp.dot(form2_far[...], cots[192:384], preferred_element_type=F32)
        for x in range(2):
            for side in range(8):
                total = hidden_grad[x, 8 * i + side] + turned(out, x, side)
                grad[x, 8 * i + side + 2] = (total * factors[x, 8 * i + side]).astype(BF16)
        acc2[...] += lax.dot_general(cots, hid3[i], NT, preferred_element_type=F32)
        cells = [
            jnp.concatenate([grad[x, 8 * i + 2 + side] for side in range(8)], axis=1) for x in range(2)
        ]
        acc1[:, 0:192] += lax.dot_general(jnp.concatenate(cells, axis=0), fields, NT, preferred_element_type=F32)

    rows = []
    for q in range(9):
        step, row = (8 - q) // 3, 32 * ((8 - q) % 3)
        terms = []
        for x in range(2):
            place = (192, 0, 96, 288)[step + x]
            terms.append(acc2[place + row : place + row + 32, 128 * x : 128 * x + 128])
        rows.append(terms[0] + terms[1])
    rows.append(acc1[0:32, 0:128] + acc1[32:64, 48:176])
    acc1[0:32, 128:144] += acc1[32:64, 176:192]
    rows.append(acc1[0:32, 128:256])
    rows.extend([jnp.zeros((32, 128), F32)] * 5)
    mine[...] = jnp.swapaxes(jnp.stack(rows, axis=0), 0, 1).reshape(16, 2, 16, 128)

    other = gx + 1 - 2 * core
    pair_copy = remote(mine.at[:, 1 - core, 0:11], got_pair, pair_sem.at[0], pair_sem.at[1], (other, gy))
    pair_copy.start()
    pair_copy.wait_recv()
    both[...] = mine[:, core, 0:11] + got_pair[...]

    def z_copy(k):
        to = down_z(k)
        return remote(both.at[pl.ds(2 * (to // 4), 2)], got_z.at[k], s1_send.at[k], s1_recv.at[k], (to, gy))

    def xy_copy(k):
        to = across(k)
        return remote(two_rows.at[lax.rem(to[0] // 2, 2)], got_xy.at[k], s2_send.at[k], s2_recv.at[k], to)

    def send_z(k, _):
        z_copy(lax.rem(k + nz // 2 - 2, nz - 1) + 1).start()
        return 0

    lax.fori_loop(1, nz, send_z, 0)

    form3_now = form3[...].astype(BF16)

    def scatter_rows(row, count):
        out = jnp.dot(form3_now, beside(grad, range(2), row, count), preferred_element_type=F32)
        for plane in range(4):
            for side in range(count):
                total = None
                for tap in range(3):
                    start = 24 * plane + 8 * tap
                    term = shift(out[start : start + 8, 128 * side : 128 * side + 128], tap - 1)
                    total = term if total is None else total + term
                part[plane, row + side] = total

    def scatter(i, _):
        scatter_rows(8 * i, 8)
        return 0

    lax.fori_loop(0, 4, scatter, 0)
    scatter_rows(32, 2)
    part_x[0] = jnp.swapaxes(part[0, 1:33], 0, 1)[0:3]
    part_x[1] = jnp.swapaxes(part[3, 1:33], 0, 1)[0:3]

    part_moves = [
        (part_x.at[0], got_x.at[1]),
        (part_x.at[1], got_x.at[0]),
        (part.at[1:3, 0], got_y.at[1]),
        (part.at[1:3, 33], got_y.at[0]),
        (part.at[0, 0], got_c.at[3]),
        (part.at[0, 33], got_c.at[2]),
        (part.at[3, 0], got_c.at[1]),
        (part.at[3, 33], got_c.at[0]),
    ]
    part_copies = [
        remote(src, dst, o_send.at[i], o_recv.at[i], places[i]) for i, (src, dst) in enumerate(part_moves)
    ]
    for copy in part_copies:
        copy.start()

    def take_z(k, total):
        z_copy(k).wait_recv()
        return total + got_z[k]

    two_rows[...] = lax.fori_loop(1, nz, take_z, both[pl.ds(2 * (gx // 4), 2)])

    def send_xy(k, _):
        xy_copy(2 * ny - k).start()
        return 0

    lax.fori_loop(1, 2 * ny, send_xy, 0)

    for copy in part_copies:
        copy.wait_recv()
    for x in range(2):
        part[x + 1, 1] += got_y[0, x]
        part[x + 1, 32] += got_y[1, x]
        part[x + 1, 1] += got_c[2 * x]
        part[x + 1, 32] += got_c[2 * x + 1]
    for x in range(2):
        grad_out[:, x] = jnp.swapaxes(part[x + 1, 1:33], 0, 1)[0:3] + got_x[x]

    def sent_z(k, _):
        z_copy(k).wait_send()
        return 0

    for copy in field_copies + cot_copies + part_copies:
        copy.wait_send()
    pair_copy.wait_send()
    lax.fori_loop(1, nz, sent_z, 0)

    def take_xy(k, total):
        xy_copy(k).wait_recv()
        return total + got_xy[k]

    total = lax.fori_loop(1, 2 * ny, take_xy, two_rows[x_hi]) * scale
    for q in range(9):
        for dz in range(3):
            second_out[3 * q + dz] = total[q : q + 1, 32 * dz : 32 * dz + 32]
        for channel in range(3):
            row, lane = 9 + q // 8, 16 * (q % 8) + 3 * channel
            first_out[channel, :, 3 * q : 3 * q + 3] = total[row : row + 1, lane : lane + 3]

    def sent_xy(k, _):
        xy_copy(k).wait_send()
        return 0

    lax.fori_loop(1, 2 * ny, sent_xy, 0)


def put_out(a, b, c, a_out, b_out, c_out):
    a_out[...] = a[...]
    b_out[...] = b[...]
    c_out[...] = c[...]


def on_device(nx, ny, field_in, conv_first, bias_first, conv_second, cotangent, mask_first, mask_second):
    scale = 1.0 / math.sqrt(2 * nx * 32 * ny * 128)
    outside = pl.BlockSpec(memory_space=pltpu.HBM)
    vmem = pl.BlockSpec(memory_space=pltpu.VMEM)
    dma = pltpu.SemaphoreType.DMA
    results = pl.pallas_call(
        functools.partial(kernel, nx, ny, scale),
        out_shape=(
            jax.ShapeDtypeStruct((3, 2, 32, 128), F32),
            jax.ShapeDtypeStruct((3, 1, 27), F32),
            jax.ShapeDtypeStruct((27, 1, 32), F32),
        ),
        in_specs=[outside] * 7,
        out_specs=(vmem, vmem, vmem),
        scratch_shapes=[
            pltpu.VMEM((32, 2, 32, 128), BF16),
            pltpu.VMEM((32, 2, 32, 128), jnp.int32),
            pltpu.VMEM((32, 2, 32, 128), jnp.int32),
            pltpu.VMEM((3, 4, 64, 128), BF16),
            pltpu.VMEM((3, 32, 27), BF16),
            pltpu.VMEM((27, 32, 32), BF16),
            pltpu.VMEM((1, 32), F32),
            pltpu.VMEM((4, 34, 32, 128), BF16),
            pltpu.VMEM((2, 32, 32, 128), F32),
            pltpu.VMEM((4, 64, 16, 128), BF16),
            pltpu.VMEM((4, 256, 1024), BF16),
            pltpu.VMEM((2, 36, 32, 128), BF16),
            pltpu.VMEM((2, 32, 32, 128), F32),
            pltpu.VMEM((384, 256), F32),
            pltpu.VMEM((64, 256), F32),
            pltpu.VMEM((64, 192), F32),
            pltpu.VMEM((192, 192), BF16),
            pltpu.VMEM((192, 192), BF16),
            pltpu.VMEM((96, 192), F32),
            pltpu.VMEM((384, 128), F32),
            pltpu.VMEM((384, 128), F32),
            pltpu.VMEM((32, 128), F32),
            pltpu.VMEM((4, 34, 8, 128), F32),
            pltpu.VMEM((2, 3, 32, 128), F32),
            pltpu.VMEM((2, 3, 32, 128), F32),
            pltpu.VMEM((2, 2, 8, 128), F32),
            pltpu.VMEM((4, 8, 128), F32),
            pltpu.VMEM((16, 2, 16, 128), F32),
            pltpu.VMEM((16, 11, 128), F32),
            pltpu.VMEM((16, 11, 128), F32),
            pltpu.VMEM((nx // 4, 2, 11, 128), F32),
            pltpu.VMEM((2, 11, 128), F32),
            pltpu.VMEM((2 * ny, 11, 128), F32),
            dma((7,)),
            dma((8,)),
            dma((8,)),
            dma((14,)),
            dma((14,)),
            dma((8,)),
            dma((8,)),
            dma((2,)),
            dma((nx // 4,)),
            dma((nx // 4,)),
            dma((2 * ny,)),
            dma((2 * ny,)),
        ],
        compiler_params=pltpu.CompilerParams(
            collective_id=0, has_side_effects=True, vmem_limit_bytes=40 * 1024 * 1024
        ),
    )(*[pltpu.with_memory_space_constraint(a, pltpu.HBM) for a in (
        cotangent, mask_first, mask_second, field_in,
        conv_first.transpose(2, 0, 1), conv_second.transpose(1, 0, 2), bias_first.reshape(1, 32),
    )])
    results = [pltpu.with_memory_space_constraint(r, pltpu.VMEM) for r in results]
    input_grad, grad_first, grad_second = pl.pallas_call(
        put_out,
        out_shape=tuple(jax.ShapeDtypeStruct(r.shape, r.dtype) for r in results),
        in_specs=[vmem] * 3,
        out_specs=(vmem,) * 3,

    )(*results)
    return input_grad, grad_first.transpose(1, 2, 0), grad_second.transpose(1, 0, 2)


def solution(mesh):
    cells = P(None, "gx", "gy", None)
    return jax.shard_map(
        functools.partial(on_device, mesh.shape["gx"], mesh.shape["gy"]),
        mesh=mesh,
        in_specs=(cells, P(), P(), P(), cells, cells, cells),
        out_specs=(cells, P("gx", None, None), P("gx", None, None)),
        check_vma=False,
    )
```

```python
import functools
import math

import jax
import jax.numpy as jnp
from jax import lax
from jax.experimental import pallas as pl
from jax.experimental.pallas import tpu as pltpu
from jax.sharding import PartitionSpec as P

MESH = pl.DeviceIdType.MESH
SLOPE = 0.01
F32 = jnp.float32
BF16 = jnp.bfloat16
NT = (((1,), (1,)), ((), ()))


def factor(mask):
    return jnp.where(mask == 1, 1.0, SLOPE).astype(F32)


def shift(values, amount):
    return pltpu.roll(values, amount % 128, 1) if amount else values


def beside(ref, planes, row, count):
    sides = []
    for side in range(count):
        blocks = []
        for plane in planes:
            block = ref[plane, pl.ds(row + side, 3)]
            blocks.append(block.reshape(block.shape[0] * block.shape[1], block.shape[2]))
        sides.append(jnp.concatenate(blocks, axis=0) if len(blocks) > 1 else blocks[0])
    return jnp.concatenate(sides, axis=1)


def kernel(
    nx, ny, scale,
    cot_in, mask1_in, mask2_in, field_in, first_in, second_in, bias_in,
    grad_out, first_out, second_out,
    cot_raw, mask1, mask2, field_raw, first_raw, second_raw, bias_raw,
    pad_cot, factors, pad_field, hid3, grad, hidden_grad, acc2, acc1,
    form1, form2, form2_far, form3, turn2, turn3, bias,
    part, part_x, got_x, got_y, got_c, mine, got_pair, both, got_z, two_rows, got_xy,
    local_sem, f_send, f_recv, p_send, p_recv, o_send, o_recv, pair_sem, s1_send, s1_recv, s2_send, s2_recv,
):
    gx = lax.axis_index("gx")
    core = lax.rem(gx, 2)
    x_hi = lax.rem(gx // 2, 2)
    nz = nx // 4
    gy = lax.axis_index("gy")

    loads = [
        pltpu.make_async_copy(cot_in, cot_raw, local_sem.at[0]),
        pltpu.make_async_copy(mask2_in, mask2, local_sem.at[1]),
        pltpu.make_async_copy(field_in, field_raw.at[:, 1:3, 16:48], local_sem.at[2]),
        pltpu.make_async_copy(mask1_in, mask1, local_sem.at[3]),
        pltpu.make_async_copy(first_in, first_raw, local_sem.at[4]),
        pltpu.make_async_copy(second_in, second_raw, local_sem.at[5]),
        pltpu.make_async_copy(bias_in, bias_raw, local_sem.at[6]),
    ]

    left, right = lax.rem(gx + nx - 1, nx), lax.rem(gx + 1, nx)
    down, up = lax.rem(gy + ny - 1, ny), lax.rem(gy + 1, ny)

    barrier = pltpu.get_barrier_semaphore()

    def down_z(k):
        return lax.rem(gx + 4 * k, nx)

    def across(k):
        return gx + 2 * (k // ny) * (1 - 2 * x_hi), lax.rem(gy + lax.rem(k, ny), ny)

    def greet_z(k, _):
        far = lax.rem(k + nz // 2 - 2, nz - 1) + 1
        pl.semaphore_signal(barrier, inc=1, device_id=(down_z(far), gy), device_id_type=MESH)
        return 0

    lax.fori_loop(1, nz, greet_z, 0)

    def greet_xy(k, _):
        pl.semaphore_signal(barrier, inc=1, device_id=across(2 * ny - k), device_id_type=MESH)
        return 0

    lax.fori_loop(1, 2 * ny, greet_xy, 0)

    for place in ((left, gy), (right, gy), (left, down), (left, up), (right, down), (right, up)):
        pl.semaphore_signal(barrier, inc=1, device_id=place, device_id_type=MESH)

    for load in loads[0:3]:
        load.start()

    loads[0].wait()
    loads[1].wait()
    for load in loads[3:7]:
        load.start()
    for x in range(2):
        for half in range(2):
            rows = slice(16 * half, 16 * half + 16)
            values = cot_raw[:, x, rows, :].astype(F32) * factor(mask2[:, x, rows, :])
            pad_cot[x + 1, 1 + 16 * half : 17 + 16 * half] = jnp.swapaxes(values, 0, 1).astype(BF16)

    loads[2].wait()
    def spread(plane, start, count):
        rows = []
        for channel in range(3):
            for dz in range(3):
                row = field_raw[channel, plane, start : start + count, :].astype(F32)
                rows.append(shift(row, 1 - dz))
        rows.extend([jnp.zeros((count, 128), F32)] * 7)
        pad_field[plane, start : start + count] = jnp.swapaxes(jnp.stack(rows, axis=0), 0, 1).astype(BF16)

    for plane in (1, 2):
        spread(plane, 16, 16)
        spread(plane, 32, 16)
    pl.semaphore_wait(barrier, 6 + (nz - 1) + (2 * ny - 1))

    def remote(src, dst, send, recv, where):
        return pltpu.make_async_remote_copy(
            src_ref=src, dst_ref=dst, send_sem=send, recv_sem=recv, device_id=where, device_id_type=MESH
        )

    places = [(left, gy), (right, gy), (gx, down), (gx, up), (left, down), (left, up), (right, down), (right, up)]
    inner = slice(16, 48)
    field_moves = [
        (field_raw.at[:, 1:2, inner], field_raw.at[:, 3:4, inner]),
        (field_raw.at[:, 2:3, inner], field_raw.at[:, 0:1, inner]),
        (pad_field.at[1:3, 16:17], pad_field.at[1:3, 48:49]),
        (pad_field.at[1:3, 47:48], pad_field.at[1:3, 15:16]),
        (pad_field.at[1:2, 16:17], pad_field.at[3:4, 48:49]),
        (pad_field.at[1:2, 47:48], pad_field.at[3:4, 15:16]),
        (pad_field.at[2:3, 16:17], pad_field.at[0:1, 48:49]),
        (pad_field.at[2:3, 47:48], pad_field.at[0:1, 15:16]),
    ]
    cuts = (1, 10, 18, 26, 33)
    chunks = [slice(cuts[i], cuts[i + 1]) for i in range(4)]
    cot_moves = [
        (pad_cot.at[1:3, 1:2], pad_cot.at[1:3, 33:34], places[2]),
        (pad_cot.at[1:3, 32:33], pad_cot.at[1:3, 0:1], places[3]),
        (pad_cot.at[1:2, 1:2], pad_cot.at[3:4, 33:34], places[4]),
        (pad_cot.at[1:2, 32:33], pad_cot.at[3:4, 0:1], places[5]),
        (pad_cot.at[2:3, 1:2], pad_cot.at[0:1, 33:34], places[6]),
        (pad_cot.at[2:3, 32:33], pad_cot.at[0:1, 0:1], places[7]),
    ]
    for chunk in chunks:
        cot_moves.append((pad_cot.at[1:2, chunk], pad_cot.at[3:4, chunk], places[0]))
        cot_moves.append((pad_cot.at[2:3, chunk], pad_cot.at[0:1, chunk], places[1]))
    field_copies = [
        remote(src, dst, f_send.at[i], f_recv.at[i], places[i]) for i, (src, dst) in enumerate(field_moves)
    ]
    cot_copies = [
        remote(src, dst, p_send.at[i], p_recv.at[i], where) for i, (src, dst, where) in enumerate(cot_moves)
    ]
    for copy in cot_copies[0:2] + field_copies + cot_copies[2:14]:
        copy.start()

    loads[4].wait()
    loads[5].wait()
    loads[6].wait()
    form1[...] = jnp.zeros_like(form1)
    form2[...] = jnp.zeros_like(form2)
    form2_far[...] = jnp.zeros_like(form2_far)
    form3[...] = jnp.zeros_like(form3)
    turn2[...] = jnp.zeros_like(turn2)
    turn3[...] = jnp.zeros_like(turn3)
    for q in range(9):
        dx, dy = q // 3, q % 3
        back2 = 32 * (8 - q)
        back3 = 32 * (3 * dx + 2 - dy)
        for dz in range(3):
            turn2[back2 : back2 + 32, 32 * dz : 32 * dz + 32] = second_raw[3 * q + dz].astype(F32)
        for channel in range(3):
            taps = first_raw[channel].astype(F32)[:, 3 * q : 3 * q + 3]
            form1[0:32, 16 * q + 3 * channel : 16 * q + 3 * channel + 3] = taps
            for dz in range(3):
                turn3[back3 : back3 + 32, 8 * dz + channel : 8 * dz + channel + 1] = taps[:, dz : dz + 1]
    form1[32:64, 48:192] = form1[0:32, 0:144]
    whole2 = jnp.transpose(turn2[...])[0:96].astype(BF16)
    form2[0:96, 0:192] = whole2[:, 96:288]
    form2[96:192, 0:192] = whole2[:, 0:192]
    form2_far[0:96, 0:96] = whole2[:, 0:96]
    form2_far[96:192, 96:192] = whole2[:, 192:288]
    whole3 = jnp.transpose(turn3[...])[0:24]
    for plane in range(4):
        for x in range(2):
            if 0 <= plane - x < 3:
                form3[24 * plane : 24 * plane + 24, 96 * x : 96 * x + 96] = whole3[:, 96 * (plane - x) : 96 * (plane - x) + 96]
    bias[...] = jnp.zeros_like(bias)
    bias[0:8, 0:32] = jnp.broadcast_to(bias_raw[...], (8, 32))
    bias[...] = jnp.broadcast_to(jnp.transpose(bias[0:8])[0:32, 0:1], (32, 128))

    loads[3].wait()
    for x in range(2):
        for half in range(2):
            rows = slice(16 * half, 16 * half + 16)
            factors[x, rows] = jnp.swapaxes(factor(mask1[:, x, rows, :]), 0, 1)

    for x in range(2):
        for rows in (slice(0, 2), slice(34, 36)):
            grad[x, rows] = jnp.zeros((2, 32, 128), BF16)
    for start in (96, 224):
        hid3[:, start : start + 32] = jnp.zeros((4, 32, 1024), BF16)

    def turned(out, x, side):
        total = None
        for tap in range(3):
            start = 96 * x + 32 * tap
            term = shift(out[start : start + 32, 128 * side : 128 * side + 128], tap - 1)
            total = term if total is None else total + term
        return total

    cot_copies[0].wait_recv()
    cot_copies[1].wait_recv()

    def backward_near(i, _):
        out = jnp.dot(form2[...], beside(pad_cot, (1, 2), 8 * i, 8), preferred_element_type=F32)
        for x in range(2):
            for side in range(8):
                hidden_grad[x, 8 * i + side] = turned(out, x, side)
        return 0

    lax.fori_loop(0, 4, backward_near, 0)

    form1_now = form1[...].astype(BF16)
    acc1[...] = jnp.zeros_like(acc1)
    acc2[...] = jnp.zeros_like(acc2)

    for copy in field_copies:
        copy.wait_recv()
    for plane in (0, 3):
        spread(plane, 16, 16)
        spread(plane, 32, 16)

    for copy in cot_copies[2:6]:
        copy.wait_recv()
    for i in range(4):
        fields = beside(pad_field, range(4), 8 * i + 15, 8)
        pre = jnp.dot(form1_now, fields, preferred_element_type=F32)
        for x in range(2):
            for side in range(8):
                lanes = slice(128 * side, 128 * side + 128)
                act = pre[32 * x : 32 * x + 32, lanes] + bias[...]
                act = jnp.where(act >= 0, act, SLOPE * act).astype(BF16).astype(F32)
                for tap in range(3):
                    start = 128 * x + 32 * tap
                    hid3[i, start : start + 32, lanes] = shift(act, 1 - tap).astype(BF16)
        for copy in cot_copies[6 + 2 * i : 8 + 2 * i]:
            copy.wait_recv()
        cots = beside(pad_cot, (1, 2, 0, 3), 8 * i, 8)
        out = jnp.dot(form2_far[...], cots[192:384], preferred_element_type=F32)
        for x in range(2):
            for side in range(8):
                total = hidden_grad[x, 8 * i + side] + turned(out, x, side)
                grad[x, 8 * i + side + 2] = (total * factors[x, 8 * i + side]).astype(BF16)
        acc2[...] += lax.dot_general(cots, hid3[i], NT, preferred_element_type=F32)
        cells = [
            jnp.concatenate([grad[x, 8 * i + 2 + side] for side in range(8)], axis=1) for x in range(2)
        ]
        acc1[:, 0:192] += lax.dot_general(jnp.concatenate(cells, axis=0), fields, NT, preferred_element_type=F32)

    rows = []
    for q in range(9):
        step, row = (8 - q) // 3, 32 * ((8 - q) % 3)
        terms = []
        for x in range(2):
            place = (192, 0, 96, 288)[step + x]
            terms.append(acc2[place + row : place + row + 32, 128 * x : 128 * x + 128])
        rows.append(terms[0] + terms[1])
    rows.append(acc1[0:32, 0:128] + acc1[32:64, 48:176])
    acc1[0:32, 128:144] += acc1[32:64, 176:192]
    rows.append(acc1[0:32, 128:256])
    rows.extend([jnp.zeros((32, 128), F32)] * 5)
    mine[...] = jnp.swapaxes(jnp.stack(rows, axis=0), 0, 1).reshape(16, 2, 16, 128)

    other = gx + 1 - 2 * core
    pair_copy = remote(mine.at[:, 1 - core, 0:11], got_pair, pair_sem.at[0], pair_sem.at[1], (other, gy))
    pair_copy.start()
    pair_copy.wait_recv()
    both[...] = mine[:, core, 0:11] + got_pair[...]

    def z_copy(k):
        to = down_z(k)
        return remote(both.at[pl.ds(2 * (to // 4), 2)], got_z.at[k], s1_send.at[k], s1_recv.at[k], (to, gy))

    def xy_copy(k):
        to = across(k)
        return remote(two_rows.at[lax.rem(to[0] // 2, 2)], got_xy.at[k], s2_send.at[k], s2_recv.at[k], to)

    def send_z(k, _):
        z_copy(lax.rem(k + nz // 2 - 2, nz - 1) + 1).start()
        return 0

    lax.fori_loop(1, nz, send_z, 0)

    form3_now = form3[...].astype(BF16)

    def scatter_rows(row, count):
        out = jnp.dot(form3_now, beside(grad, range(2), row, count), preferred_element_type=F32)
        for plane in range(4):
            for side in range(count):
                total = None
                for tap in range(3):
                    start = 24 * plane + 8 * tap
                    term = shift(out[start : start + 8, 128 * side : 128 * side + 128], tap - 1)
                    total = term if total is None else total + term
                part[plane, row + side] = total

    def scatter(i, _):
        scatter_rows(8 * i, 8)
        return 0

    lax.fori_loop(0, 4, scatter, 0)
    scatter_rows(32, 2)
    part_x[0] = jnp.swapaxes(part[0, 1:33], 0, 1)[0:3]
    part_x[1] = jnp.swapaxes(part[3, 1:33], 0, 1)[0:3]

    part_moves = [
        (part_x.at[0], got_x.at[1]),
        (part_x.at[1], got_x.at[0]),
        (part.at[1:3, 0], got_y.at[1]),
        (part.at[1:3, 33], got_y.at[0]),
        (part.at[0, 0], got_c.at[3]),
        (part.at[0, 33], got_c.at[2]),
        (part.at[3, 0], got_c.at[1]),
        (part.at[3, 33], got_c.at[0]),
    ]
    part_copies = [
        remote(src, dst, o_send.at[i], o_recv.at[i], places[i]) for i, (src, dst) in enumerate(part_moves)
    ]
    for copy in part_copies:
        copy.start()

    def take_z(k, total):
        z_copy(k).wait_recv()
        return total + got_z[k]

    two_rows[...] = lax.fori_loop(1, nz, take_z, both[pl.ds(2 * (gx // 4), 2)])

    def send_xy(k, _):
        xy_copy(2 * ny - k).start()
        return 0

    lax.fori_loop(1, 2 * ny, send_xy, 0)

    for copy in part_copies:
        copy.wait_recv()
    for x in range(2):
        part[x + 1, 1] += got_y[0, x]
        part[x + 1, 32] += got_y[1, x]
        part[x + 1, 1] += got_c[2 * x]
        part[x + 1, 32] += got_c[2 * x + 1]
    for x in range(2):
        grad_out[:, x] = jnp.swapaxes(part[x + 1, 1:33], 0, 1)[0:3] + got_x[x]

    def sent_z(k, _):
        z_copy(k).wait_send()
        return 0

    for copy in field_copies + cot_copies + part_copies:
        copy.wait_send()
    pair_copy.wait_send()
    lax.fori_loop(1, nz, sent_z, 0)

    def take_xy(k, total):
        xy_copy(k).wait_recv()
        return total + got_xy[k]

    total = lax.fori_loop(1, 2 * ny, take_xy, two_rows[x_hi]) * scale
    for q in range(9):
        for dz in range(3):
            second_out[3 * q + dz] = total[q : q + 1, 32 * dz : 32 * dz + 32]
        for channel in range(3):
            row, lane = 9 + q // 8, 16 * (q % 8) + 3 * channel
            first_out[channel, :, 3 * q : 3 * q + 3] = total[row : row + 1, lane : lane + 3]

    def sent_xy(k, _):
        xy_copy(k).wait_send()
        return 0

    lax.fori_loop(1, 2 * ny, sent_xy, 0)


def put_out(a, b, c, a_out, b_out, c_out, sem):
    pairs = ((a, a_out), (b, b_out), (c, c_out))
    copies = [pltpu.make_async_copy(src, dst, sem.at[i]) for i, (src, dst) in enumerate(pairs)]
    for copy in copies:
        copy.start()
    for copy in copies:
        copy.wait()


def on_device(nx, ny, field_in, conv_first, bias_first, conv_second, cotangent, mask_first, mask_second):
    scale = 1.0 / math.sqrt(2 * nx * 32 * ny * 128)
    outside = pl.BlockSpec(memory_space=pltpu.HBM)
    vmem = pl.BlockSpec(memory_space=pltpu.VMEM)
    dma = pltpu.SemaphoreType.DMA
    results = pl.pallas_call(
        functools.partial(kernel, nx, ny, scale),
        out_shape=(
            jax.ShapeDtypeStruct((3, 2, 32, 128), F32),
            jax.ShapeDtypeStruct((3, 1, 27), F32),
            jax.ShapeDtypeStruct((27, 1, 32), F32),
        ),
        in_specs=[outside] * 7,
        out_specs=(vmem, vmem, vmem),
        scratch_shapes=[
            pltpu.VMEM((32, 2, 32, 128), BF16),
            pltpu.VMEM((32, 2, 32, 128), jnp.int32),
            pltpu.VMEM((32, 2, 32, 128), jnp.int32),
            pltpu.VMEM((3, 4, 64, 128), BF16),
            pltpu.VMEM((3, 32, 27), BF16),
            pltpu.VMEM((27, 32, 32), BF16),
            pltpu.VMEM((1, 32), F32),
            pltpu.VMEM((4, 34, 32, 128), BF16),
            pltpu.VMEM((2, 32, 32, 128), F32),
            pltpu.VMEM((4, 64, 16, 128), BF16),
            pltpu.VMEM((4, 256, 1024), BF16),
            pltpu.VMEM((2, 36, 32, 128), BF16),
            pltpu.VMEM((2, 32, 32, 128), F32),
            pltpu.VMEM((384, 256), F32),
            pltpu.VMEM((64, 256), F32),
            pltpu.VMEM((64, 192), F32),
            pltpu.VMEM((192, 192), BF16),
            pltpu.VMEM((192, 192), BF16),
            pltpu.VMEM((96, 192), F32),
            pltpu.VMEM((384, 128), F32),
            pltpu.VMEM((384, 128), F32),
            pltpu.VMEM((32, 128), F32),
            pltpu.VMEM((4, 34, 8, 128), F32),
            pltpu.VMEM((2, 3, 32, 128), F32),
            pltpu.VMEM((2, 3, 32, 128), F32),
            pltpu.VMEM((2, 2, 8, 128), F32),
            pltpu.VMEM((4, 8, 128), F32),
            pltpu.VMEM((16, 2, 16, 128), F32),
            pltpu.VMEM((16, 11, 128), F32),
            pltpu.VMEM((16, 11, 128), F32),
            pltpu.VMEM((nx // 4, 2, 11, 128), F32),
            pltpu.VMEM((2, 11, 128), F32),
            pltpu.VMEM((2 * ny, 11, 128), F32),
            dma((7,)),
            dma((8,)),
            dma((8,)),
            dma((14,)),
            dma((14,)),
            dma((8,)),
            dma((8,)),
            dma((2,)),
            dma((nx // 4,)),
            dma((nx // 4,)),
            dma((2 * ny,)),
            dma((2 * ny,)),
        ],
        compiler_params=pltpu.CompilerParams(
            collective_id=0, has_side_effects=True, vmem_limit_bytes=40 * 1024 * 1024
        ),
    )(*[pltpu.with_memory_space_constraint(a, pltpu.HBM) for a in (
        cotangent, mask_first, mask_second, field_in,
        conv_first.transpose(2, 0, 1), conv_second.transpose(1, 0, 2), bias_first.reshape(1, 32),
    )])
    results = [pltpu.with_memory_space_constraint(r, pltpu.VMEM) for r in results]
    input_grad, grad_first, grad_second = pl.pallas_call(
        put_out,
        out_shape=tuple(jax.ShapeDtypeStruct(r.shape, r.dtype) for r in results),
        in_specs=[vmem] * 3,
        out_specs=(outside,) * 3,
        scratch_shapes=[dma((3,))],

    )(*results)
    return input_grad, grad_first.transpose(1, 2, 0), grad_second.transpose(1, 0, 2)


def solution(mesh):
    cells = P(None, "gx", "gy", None)
    return jax.shard_map(
        functools.partial(on_device, mesh.shape["gx"], mesh.shape["gy"]),
        mesh=mesh,
        in_specs=(cells, P(), P(), P(), cells, cells, cells),
        out_specs=(cells, P("gx", None, None), P("gx", None, None)),
        check_vma=False,
    )
```
